128 devices in a mesh: grp: 8 (over x, y_hi), shard: 16 (over z, y_lo, core).
Axes of the slice: x: 4, y: 4 (y_hi: 2, y_lo: 2; y = y_hi * 2 + y_lo), z: 4, core: 2. Of those that a mesh axis runs over, the one named last changes fastest.
Arguments:
- points: bfloat16 [8, 24576, 1024], P('grp', 'shard'), may hold values from -6 to 6
- centroids: bfloat16 [8, 1024, 1024], P('grp', 'shard'), may hold values from -1.5 to 1.5
- tile_counts: int32 [8], replicated, may hold values from 97 to 192, as said below
Outputs:
- new_centroids: float32 [8, 1024, 1024], P('grp', 'shard')
- posterior_rows: bfloat16 [8, 24576, 1024], P('grp', 'shard')
The draws below stay inside these ranges and needn't reach their ends.
Inputs may be any that keep to these rules, and one draw needn't show every extreme that they name: `tile_counts`: every coarse cluster has more than half of its 192 tile slots live, and some cluster has all 192.
All inputs are finite; a program needn't handle non-finite values.
Results may differ from the reference program's by a relative error of at most 0.0076.
Values may be sent and summed in bfloat16 or wider, within the bound.
A program may use at most 64 MiB of HBM per device.

```python
import jax
import jax.numpy as jnp
from jax import lax

EMBED_WIDTH = 1024
K = 1024
TILE = 128
POINTS_DEV = 1536
ITERS = 2
CLUSTERS = 8
ROWS = 24576
MAXTILES = 192
N_SHARD = 16


def draw_tile_counts(key, part):
    count_key = jax.random.fold_in(key, 11)
    place_key = jax.random.fold_in(key, 23)
    counts = jax.random.randint(count_key, (CLUSTERS,), MAXTILES // 2 + 1, MAXTILES + 1, dtype=jnp.int32)
    full_place = jax.random.randint(place_key, (), 0, CLUSTERS, dtype=jnp.int32)
    positions = jnp.arange(CLUSTERS, dtype=jnp.int32)
    return jnp.where(positions == full_place, MAXTILES, counts).astype(jnp.int32)


def block_scale(own_key, shape, split, smallest, top_value):
    def one(dim, parts):
        draws = jax.random.uniform(jax.random.fold_in(jax.random.fold_in(own_key, 6), dim), (parts,), jnp.float32, smallest / len(split), top_value / len(split))
        return jnp.repeat(jnp.exp(draws), shape[dim] // parts).reshape((-1,) + (1,) * (len(shape) - dim - 1))

    gain = one(*split[0])
    for cut in split[1:]:
        gain = gain * one(*cut)
    return gain


def bell_draw(rng, dims, spread, bound, split=(), kind=jnp.bfloat16):
    entries = jax.random.normal(rng, dims, jnp.float32) * spread
    if len(split) > 0:
        entries = block_scale(rng, dims, split, -0.22, 0.18) * entries
    return jnp.clip(entries, min=-bound, max=bound).astype(kind)


def setup_inputs(seed: int = 0) -> dict:
    key_list = jax.random.split(jax.random.key(seed), 4)
    return {
        "points": bell_draw(key_list[0], (CLUSTERS, ROWS, EMBED_WIDTH), 1.0, 6.0, ((0, 8), (1, 16))),
        "centroids": jnp.clip(jax.random.uniform(key_list[1], (CLUSTERS, K, EMBED_WIDTH), jnp.float32, -1.5, 1.5) * block_scale(key_list[1], (CLUSTERS, K, EMBED_WIDTH), ((0, 8), (1, 16)), -0.4, 0.0), -1.5, 1.5).astype(jnp.bfloat16),
        "tile_counts": draw_tile_counts(jax.random.fold_in(key_list[3], 71), 0),
    }


sharpness_factor = 48.0
epsilon = 1e-06

def rms_unit(values):
    return values * lax.rsqrt(lax.optimization_barrier(jnp.mean(values * values, axis=-1, keepdims=True)) + epsilon)

def one_cluster(clustering_arguments):
    cluster_points, start_table, tile_total = clustering_arguments
    row_index = jnp.arange(ROWS, dtype=jnp.int32)
    tile_number = row_index % POINTS_DEV // TILE * N_SHARD + row_index // POINTS_DEV
    valid_rows = (tile_number < tile_total).astype(jnp.float32)
    unit_embeddings = rms_unit(cluster_points.astype(jnp.float32)).astype(jnp.bfloat16)
    present_centroids = start_table
    updated = jnp.zeros((K, EMBED_WIDTH), jnp.float32)
    mean_rows = jnp.zeros((ROWS, EMBED_WIDTH), jnp.bfloat16)
    for iteration in range(ITERS):
        affinity_scores = lax.dot_general(unit_embeddings, present_centroids, (((1,), (1,)), ((), ())), preferred_element_type=jnp.float32) * (sharpness_factor / EMBED_WIDTH)
        exponent_terms = jnp.exp(affinity_scores)
        weights = exponent_terms / lax.optimization_barrier(jnp.sum(exponent_terms, axis=-1, keepdims=True)) * valid_rows[:, None]
        weights = weights.astype(jnp.bfloat16)
        centroid_sums = lax.dot_general(weights, unit_embeddings, (((0,), (0,)), ((), ())), preferred_element_type=jnp.float32)
        if iteration == ITERS - 1:
            mean_rows = jnp.dot(weights, present_centroids, preferred_element_type=jnp.float32).astype(jnp.bfloat16)
        updated = rms_unit(centroid_sums)
        present_centroids = updated.astype(jnp.bfloat16)
    return (updated, mean_rows)

def reference(points, centroids, tile_counts):
    new_centroids, posterior_rows = lax.map(one_cluster, (points, centroids, tile_counts))
    return (new_centroids, posterior_rows)
```

```python
import functools
import math

import jax
import jax.numpy as jnp
from jax import lax
from jax.experimental import pallas as pl
from jax.experimental.pallas import tpu as pltpu
from jax.sharding import PartitionSpec as P

MESH = pl.DeviceIdType.MESH
TILE = 128
ITERS = 2
EPS = 1e-06
SHARP = 48.0
Q = 2
F32 = jnp.float32
BF16 = jnp.bfloat16
N_SEMS = 128


def kernel(
    counts, points, cents, newc, post,
    pts, n, e, den, inv, tab, acc, ssnd, srcv, x, r1, r2, r3, ctr, pout,
    send, recv, lsem,
):
    rows_all, width = n.shape
    per = tab.shape[4]
    half = per // 2
    g = lax.axis_index("grp")
    sh = lax.axis_index("shard")
    z, y, c = sh // 4, (sh // 2) % 2, sh % 2

    def peer(dz, dy, dc):
        zz = (z + dz) % 4
        yy = (y + dy) % 2
        cc = (c + dc) % 2
        return (g, zz * 4 + yy * 2 + cc)

    zp, zm, yo, sib = peer(1, 0, 0), peer(3, 0, 0), peer(0, 1, 0), peer(0, 0, 1)

    copies = {}

    def start(key, src, dst, dev):
        i = len(copies)
        cp = pltpu.make_async_remote_copy(
            src_ref=src, dst_ref=dst, send_sem=send.at[i], recv_sem=recv.at[i],
            device_id=dev, device_id_type=MESH,
        )
        cp.start()
        copies[key] = cp

    def got(*key):
        copies[key].wait_recv()

    parts = 4
    prow = rows_all // parts
    loads = []
    for i in range(parts):
        cp = pltpu.make_async_copy(
            points.at[0, pl.ds(i * prow, prow)], pts.at[pl.ds(i * prow, prow)], lsem.at[i]
        )
        cp.start()
        loads.append(cp)
    own_loads = []
    for q in range(Q):
        cp = pltpu.make_async_copy(
            cents.at[0, pl.ds(q * per, per)], tab.at[0, 0, q, 0], lsem.at[parts + q]
        )
        cp.start()
        own_loads.append(cp)

    barrier = pltpu.get_barrier_semaphore()
    for dev in (zp, zm, yo, sib):
        pl.semaphore_signal(barrier, inc=1, device_id=dev, device_id_type=MESH)
    pl.semaphore_wait(barrier, 4)

    def ag_own(it, q, src):
        start((it, q, "zp"), src, tab.at[it, 3, q, 0], zp)
        start((it, q, "zm"), src, tab.at[it, 2, q, 0], zm)
        start((it, q, "y"), src, tab.at[it, 1, q, 0], yo)
        start((it, q, "s0"), src, tab.at[it, 0, q, 1], sib)

    def ag_relay_a(it, q):
        got(it, q, "zp")
        start((it, q, "hzp"), tab.at[it, 3, q, 0, pl.ds(0, half)], tab.at[it, 4, q, 0, pl.ds(0, half)], zp)
        got(it, q, "zm")
        start((it, q, "hzm"), tab.at[it, 2, q, 0, pl.ds(half, half)], tab.at[it, 4, q, 0, pl.ds(half, half)], zm)
        got(it, q, "y")
        start((it, q, "s1"), tab.at[it, pl.ds(1, 3), q, 0], tab.at[it, pl.ds(1, 3), q, 1], sib)

    def ag_relay_b(it, q):
        start((it, q, "yzp"), tab.at[it, 1, q, 0], tab.at[it, 6, q, 0], zp)
        start((it, q, "yzm"), tab.at[it, 1, q, 0], tab.at[it, 5, q, 0], zm)

    def ag_relay_c(it, q):
        got(it, q, "hzp")
        got(it, q, "hzm")
        start((it, q, "hy"), tab.at[it, 4, q, 0], tab.at[it, 7, q, 0], yo)
        start((it, q, "s2"), tab.at[it, 4, q, 0], tab.at[it, 4, q, 1], sib)

    def ag_relay_d(it, q):
        got(it, q, "yzp")
        got(it, q, "yzm")
        got(it, q, "hy")
        start((it, q, "s3"), tab.at[it, pl.ds(5, 3), q, 0], tab.at[it, pl.ds(5, 3), q, 1], sib)

    scale = SHARP / width * math.log2(math.e)

    def logits(it, p0, p1, q0, q1, first=False):
        m = (p1 - p0) * (q1 - q0) * 2 * per

        def step(rt, carry):
            at = pl.ds(pl.multiple_of(rt * 256, 256), 256)
            s = lax.dot_general(
                tab[it, p0:p1, q0:q1].reshape(m, width), n[at, :],
                (((1,), (1,)), ((), ())), preferred_element_type=F32,
            )
            ex = jnp.exp2(s * scale)
            part = jnp.sum(ex.reshape(m // 8, 8, 256), axis=0)
            den[:, at] = part if first else den[:, at] + part
            e[p0:p1, q0:q1, :, :, at] = ex.astype(BF16).reshape(p1 - p0, q1 - q0, 2, per, 256)
            return carry

        lax.fori_loop(0, rows_all // 256, step, 0)

    def invert():
        for t in range(rows_all // TILE):
            at = slice(t * TILE, (t + 1) * TILE)
            live = (t * 16 + sh < counts[g]).astype(F32)
            inv[:, at] = live / jnp.sum(den[:, at], axis=0, keepdims=True)

    def weigh(p0, p1, q0, q1):
        m = (p1 - p0) * (q1 - q0) * 2 * per

        def step(j, carry):
            at = pl.ds(pl.multiple_of(j * 256, 256), 256)
            v = e[p0:p1, q0:q1, :, :, at].reshape(m, 256).astype(F32) * inv[:, at]
            e[p0:p1, q0:q1, :, :, at] = v.astype(BF16).reshape(p1 - p0, q1 - q0, 2, per, 256)
            return carry

        lax.fori_loop(0, rows_all // 256, step, 0)

    def sums(it, p0, p1, q0, q1):
        weigh(p0, p1, q0, q1)
        m = (p1 - p0) * (q1 - q0) * 2 * per

        def step(ft, carry):
            at = pl.ds(pl.multiple_of(ft * 256, 256), 256)
            s = jnp.dot(
                e[p0:p1, q0:q1].reshape(m, rows_all), n[:, at], preferred_element_type=F32
            ).reshape(p1 - p0, q1 - q0, 2, per, 256)
            acc[p0:p1, q0:q1, :, at] = s[:, :, 0]
            ssnd[it, p0:p1, q0:q1, :, at] = s[:, :, 1].astype(BF16)
            return carry

        lax.fori_loop(0, width // 256, step, 0)
        for q in range(q0, q1):
            start((it, q, "x", p0), ssnd.at[it, pl.ds(p0, p1 - p0), q], srcv.at[it, pl.ds(p0, p1 - p0), q], sib)

    def base(it, p, q, rows=slice(None)):
        return acc[p, q, rows] + srcv[it, p, q, rows].astype(F32)

    def rs_one(it, q):
        got(it, q, "x", 5)
        for p, dev in ((5, zp), (6, zm), (7, yo)):
            x[it, p, q] = base(it, p, q).astype(BF16)
            start((it, q, "r1", p - 5), x.at[it, p, q], r1.at[it, p - 5, q], dev)

    lo, hi = slice(0, half), slice(half, 2 * half)

    def rs_two(it, q):
        got(it, q, "x", 2)
        got(it, q, "r1", 2)
        x[it, 4, q] = (base(it, 4, q) + r1[it, 2, q].astype(F32)).astype(BF16)
        start((it, q, "r2", 0), x.at[it, 4, q, pl.ds(0, half)], r2.at[it, 0, q], zm)
        start((it, q, "r2", 1), x.at[it, 4, q, pl.ds(half, half)], r2.at[it, 1, q], zp)
        got(it, q, "x", 0)
        got(it, q, "r1", 0)
        got(it, q, "r1", 1)
        x[it, 1, q] = (base(it, 1, q) + r1[it, 0, q].astype(F32) + r1[it, 1, q].astype(F32)).astype(BF16)
        start((it, q, "r3", 2), x.at[it, 1, q], r3.at[it, 2, q], yo)
        x[it, 3, q, hi] = base(it, 3, q, hi).astype(BF16)
        start((it, q, "r3e", 0), x.at[it, 3, q, pl.ds(half, half)], r3.at[it, 0, q, pl.ds(half, half)], zm)
        x[it, 2, q, lo] = base(it, 2, q, lo).astype(BF16)
        start((it, q, "r3e", 1), x.at[it, 2, q, pl.ds(0, half)], r3.at[it, 1, q, pl.ds(0, half)], zp)

    def rs_three(it, q):
        got(it, q, "r2", 0)
        x[it, 3, q, lo] = (base(it, 3, q, lo) + r2[it, 0, q].astype(F32)).astype(BF16)
        start((it, q, "r3", 0), x.at[it, 3, q, pl.ds(0, half)], r3.at[it, 0, q, pl.ds(0, half)], zm)
        got(it, q, "r2", 1)
        x[it, 2, q, hi] = (base(it, 2, q, hi) + r2[it, 1, q].astype(F32)).astype(BF16)
        start((it, q, "r3", 1), x.at[it, 2, q, pl.ds(half, half)], r3.at[it, 1, q, pl.ds(half, half)], zp)

    def rs_last(it, q):
        for key in (("r3", 2), ("r3e", 0), ("r3e", 1), ("r3", 0), ("r3", 1)):
            got(it, q, *key)
        s = base(it, 0, q)
        for i in range(3):
            s = s + r3[it, i, q].astype(F32)
        s = s * lax.rsqrt(jnp.mean(s * s, axis=-1, keepdims=True) + EPS)
        return s

    def post_tiles(t0, t1):
        def step(t, carry):
            at = pl.ds(pl.multiple_of(t * 256, 256), 256)
            w = e[:, :, :, :, at].reshape(16 * Q * per, 256)
            pout[at, :] = lax.dot_general(
                w, tab[ITERS - 1].reshape(16 * Q * per, width),
                (((0,), (0,)), ((), ())), preferred_element_type=F32,
            ).astype(BF16)
            return carry

        lax.fori_loop(t0, t1, step, 0)
        cp = pltpu.make_async_copy(
            pout.at[pl.ds(t0 * 256, (t1 - t0) * 256)],
            post.at[0, pl.ds(t0 * 256, (t1 - t0) * 256)], lsem.at[parts + Q + t0],
        )
        cp.start()
        return cp

    for q in range(Q):
        ag_own(0, q, cents.at[0, pl.ds(q * per, per)])

    def unit(j, carry):
        at = pl.ds(pl.multiple_of(j * 32, 32), 32)
        v = pts[at, :].astype(F32)
        n[at, :] = (v * lax.rsqrt(jnp.mean(v * v, axis=-1, keepdims=True) + EPS)).astype(BF16)
        return carry

    for i in range(parts):
        loads[i].wait()
        lax.fori_loop(i * prow // 32, (i + 1) * prow // 32, unit, 0)
    for cp in own_loads:
        cp.wait()

    outs = []
    for it in range(ITERS):
        last = it == ITERS - 1
        for q in range(Q):
            got(it, q, "s0")
        logits(it, 0, 1, 0, Q, first=True)
        for q in range(Q):
            ag_relay_a(it, q)
        for q in range(Q):
            ag_relay_b(it, q)
        for q in range(Q):
            got(it, q, "s1")
        logits(it, 1, 4, 0, Q)
        for q in range(Q):
            ag_relay_c(it, q)
        for q in range(Q):
            ag_relay_d(it, q)
            got(it, q, "s2")
            got(it, q, "s3")
            logits(it, 4, 8, q, q + 1)
        invert()
        for q in range(Q):
            sums(it, 5, 8, q, q + 1)
        for q in range(Q):
            sums(it, 2, 5, q, q + 1)
            rs_one(it, q)
        sums(it, 0, 2, 0, Q)
        if last:
            outs.append(post_tiles(0, 2))
        for q in range(Q):
            rs_two(it, q)
            if last:
                outs.append(post_tiles(2 + q, 3 + q))
        if last:
            outs.append(post_tiles(4, 6))
        for q in range(Q):
            rs_three(it, q)
        for q in range(Q):
            s = rs_last(it, q)
            if last:
                ctr[q] = s
                cp = pltpu.make_async_copy(
                    ctr.at[q], newc.at[0, pl.ds(q * per, per)], lsem.at[parts + q]
                )
                cp.start()
                outs.append(cp)
            else:
                tab[it + 1, 0, q, 0] = s.astype(BF16)
                ag_own(it + 1, q, tab.at[it + 1, 0, q, 0])
    for cp in copies.values():
        cp.wait_send()
    for cp in outs:
        cp.wait()


def body(points, centroids, tile_counts):
    rows, width = points.shape[1:]
    mine = centroids.shape[1]
    k = mine * 16
    per = mine // Q
    dma = pltpu.SemaphoreType.DMA
    scratch = [
        pltpu.VMEM((rows, width), BF16),
        pltpu.VMEM((rows, width), BF16),
        pltpu.VMEM((8, Q, 2, per, rows), BF16),
        pltpu.VMEM((8, rows), F32),
        pltpu.VMEM((1, rows), F32),
        pltpu.VMEM((ITERS, 8, Q, 2, per, width), BF16),
        pltpu.VMEM((8, Q, per, width), F32),
        pltpu.VMEM((ITERS, 8, Q, per, width), BF16),
        pltpu.VMEM((ITERS, 8, Q, per, width), BF16),
        pltpu.VMEM((ITERS, 8, Q, per, width), BF16),
        pltpu.VMEM((ITERS, 3, Q, per, width), BF16),
        pltpu.VMEM((ITERS, 2, Q, per // 2, width), BF16),
        pltpu.VMEM((ITERS, 3, Q, per, width), BF16),
        pltpu.VMEM((Q, per, width), F32),
        pltpu.VMEM((rows, width), BF16),
        dma((N_SEMS,)), dma((N_SEMS,)), dma((16,)),
    ]
    anyspace = pl.BlockSpec(memory_space=pl.ANY)
    return pl.pallas_call(
        kernel,
        out_shape=(
            jax.ShapeDtypeStruct((1, mine, width), F32),
            jax.ShapeDtypeStruct((1, rows, width), BF16),
        ),
        in_specs=[pl.BlockSpec(memory_space=pltpu.SMEM), anyspace, anyspace],
        out_specs=(anyspace, anyspace),
        scratch_shapes=scratch,
        compiler_params=pltpu.CompilerParams(
            collective_id=0, has_side_effects=True, vmem_limit_bytes=60 * 1024 * 1024
        ),
    )(tile_counts, points, centroids)


def solution(mesh):
    return jax.shard_map(
        body,
        mesh=mesh,
        in_specs=(P("grp", "shard", None), P("grp", "shard", None), P()),
        out_specs=(P("grp", "shard", None), P("grp", "shard", None)),
        check_vma=False,
    )
```

```python
import math

import jax
import jax.numpy as jnp
from jax import lax
from jax.experimental import pallas as pl
from jax.experimental.pallas import tpu as pltpu
from jax.sharding import PartitionSpec as P

MESH = pl.DeviceIdType.MESH
TILE = 128
ITERS = 2
EPS = 1e-06
SHARP = 48.0
Q = 4
F32 = jnp.float32
BF16 = jnp.bfloat16
N_SEMS = 192
VLIM = 30
UNROLL = 2
YO, ZP1, ZM1, OWN, ZZ = 0, 1, 2, 3, 4


def kernel(
    counts_in, points, cents, newc, post,
    counts, pts, n, e, den, inv, tab, acc, ssnd, srcv, x, r1, r2, r3, ctr, pout,
    send, recv, lsem,
):
    rows_all, width = n.shape
    per = tab.shape[4]
    g = lax.axis_index("grp")
    sh = lax.axis_index("shard")
    z, y, c = sh // 4, (sh // 2) % 2, sh % 2

    def peer(dz, dy, dc):
        zz = (z + dz) % 4
        yy = (y + dy) % 2
        cc = (c + dc) % 2
        return (g, zz * 4 + yy * 2 + cc)

    zp, zm, yo, sib = peer(1, 0, 0), peer(3, 0, 0), peer(0, 1, 0), peer(0, 0, 1)

    copies = {}
    drained = set()

    def start(key, src, dst, dev):
        i = len(copies)
        cp = pltpu.make_async_remote_copy(
            src_ref=src, dst_ref=dst, send_sem=send.at[i], recv_sem=recv.at[i],
            device_id=dev, device_id_type=MESH,
        )
        cp.start()
        copies[key] = cp

    def got(*key):
        copies[key].wait_recv()

    def drain():
        for key, cp in copies.items():
            if key not in drained:
                cp.wait_send()
                drained.add(key)

    parts = 4
    prow = rows_all // parts
    loads = []
    for i in range(parts):
        cp = pltpu.make_async_copy(
            points.at[0, pl.ds(i * prow, prow)], pts.at[pl.ds(i * prow, prow)], lsem.at[i]
        )
        cp.start()
        loads.append(cp)
    for q in range(Q):
        cp = pltpu.make_async_copy(
            cents.at[0, pl.ds(q * per, per)], tab.at[0, OWN, q, 0], lsem.at[parts + q]
        )
        cp.start()
        loads.append(cp)

    cp = pltpu.make_async_copy(counts_in, counts, lsem.at[15])
    cp.start()
    loads.append(cp)

    barrier = pltpu.get_barrier_semaphore()
    for dev in (zp, zm, yo, sib):
        pl.semaphore_signal(barrier, inc=1, device_id=dev, device_id_type=MESH)
    pl.semaphore_wait(barrier, 4)

    def ag_own(it, q, src):
        start((it, q, "zp"), src, tab.at[it, ZM1, q, 0], zp)
        start((it, q, "zm"), src, tab.at[it, ZP1, q, 0], zm)
        start((it, q, "y"), src, tab.at[it, YO, q, 0], yo)
        start((it, q, "s0"), src, tab.at[it, OWN, q, 1], sib)

    def ag_a(it, q):
        got(it, q, "zp")
        if q % 2 == 0:
            start((it, q, "h"), tab.at[it, ZM1, q, 0], tab.at[it, ZZ, q, 0], zp)
        got(it, q, "zm")
        if q % 2 == 1:
            start((it, q, "h"), tab.at[it, ZP1, q, 0], tab.at[it, ZZ, q, 0], zm)
        got(it, q, "y")
        start((it, q, "s1"), tab.at[it, pl.ds(0, 3), q, 0], tab.at[it, pl.ds(0, 3), q, 1], sib)

    def ag_b(it, q):
        start((it, q, "yzp"), tab.at[it, YO, q, 0], tab.at[it, 6, q, 0], zp)
        start((it, q, "yzm"), tab.at[it, YO, q, 0], tab.at[it, 5, q, 0], zm)

    def ag_c(it, q):
        got(it, q, "h")
        start((it, q, "hy"), tab.at[it, ZZ, q, 0], tab.at[it, 7, q, 0], yo)
        start((it, q, "s2"), tab.at[it, ZZ, q, 0], tab.at[it, ZZ, q, 1], sib)

    def ag_d(it, q):
        got(it, q, "yzp")
        got(it, q, "yzm")
        start((it, q, "s3"), tab.at[it, pl.ds(5, 2), q, 0], tab.at[it, pl.ds(5, 2), q, 1], sib)

    def ag_e(it, q):
        got(it, q, "hy")
        start((it, q, "s4"), tab.at[it, 7, q, 0], tab.at[it, 7, q, 1], sib)

    scale = SHARP / width * math.log2(math.e)
    n_rt = rows_all // 256

    def logits(it, p0, p1, q0, q1, t0=0, t1=n_rt, first=False):
        m = (p1 - p0) * (q1 - q0) * 2 * per

        def step(rt, carry):
            at = pl.ds(pl.multiple_of(rt * 256, 256), 256)
            s = lax.dot_general(
                tab[it, p0:p1, q0:q1].reshape(m, width), n[at, :],
                (((1,), (1,)), ((), ())), preferred_element_type=F32,
            )
            ex = jnp.exp2(s * scale)
            part = jnp.sum(ex.reshape(m // 8, 8, 256), axis=0)
            den[:, at] = part if first else den[:, at] + part
            e[p0:p1, q0:q1, :, :, at] = ex.astype(BF16).reshape(p1 - p0, q1 - q0, 2, per, 256)
            return carry

        lax.fori_loop(t0, t1, step, 0, unroll=UNROLL)

    def invert():
        for t in range(rows_all // TILE):
            at = slice(t * TILE, (t + 1) * TILE)
            live = (t * 16 + sh < counts[g]).astype(F32)
            inv[:, at] = live / jnp.sum(den[:, at], axis=0, keepdims=True)

    def sums(it, p0, p1, q0, q1):
        m = (p1 - p0) * (q1 - q0) * 2 * per

        def weigh(j, carry):
            at = pl.ds(pl.multiple_of(j * 256, 256), 256)
            v = e[p0:p1, q0:q1, :, :, at].reshape(m, 256).astype(F32) * inv[:, at]
            e[p0:p1, q0:q1, :, :, at] = v.astype(BF16).reshape(p1 - p0, q1 - q0, 2, per, 256)
            return carry

        lax.fori_loop(0, n_rt, weigh, 0, unroll=UNROLL)

        def step(ft, carry):
            at = pl.ds(pl.multiple_of(ft * 256, 256), 256)
            s = jnp.dot(
                e[p0:p1, q0:q1].reshape(m, rows_all), n[:, at], preferred_element_type=F32
            ).reshape(p1 - p0, q1 - q0, 2, per, 256)
            acc[p0:p1, q0:q1, :, at] = s[:, :, 0]
            ssnd[it, p0:p1, q0:q1, :, at] = s[:, :, 1].astype(BF16)
            return carry

        lax.fori_loop(0, width // 256, step, 0, unroll=UNROLL)
        for q in range(q0, q1):
            start((it, q, "x", p0), ssnd.at[it, pl.ds(p0, p1 - p0), q], srcv.at[it, pl.ds(p0, p1 - p0), q], sib)

    def base(it, p, q):
        return acc[p, q] + srcv[it, p, q].astype(F32)

    def rs_one(it, q):
        got(it, q, "x", 5)
        for p, dev in ((5, zp), (6, zm), (7, yo)):
            x[it, p, q] = base(it, p, q).astype(BF16)
            start((it, q, "r1", p - 5), x.at[it, p, q], r1.at[it, p - 5, q], dev)

    def rs_two(it, q):
        got(it, q, "x", 3)
        got(it, q, "r1", 2)
        x[it, ZZ, q] = (base(it, ZZ, q) + r1[it, 2, q].astype(F32)).astype(BF16)
        start((it, q, "r2"), x.at[it, ZZ, q], r2.at[it, q], zm if q % 2 == 0 else zp)

    def rs_early(it, q):
        got(it, q, "x", 0)
        p, slot, dev = (ZP1, 1, zp) if q % 2 == 0 else (ZM1, 0, zm)
        x[it, p, q] = base(it, p, q).astype(BF16)
        start((it, q, "r3", slot), x.at[it, p, q], r3.at[it, slot, q], dev)

    def rs_y(it, q):
        got(it, q, "r1", 0)
        got(it, q, "r1", 1)
        x[it, YO, q] = (base(it, YO, q) + r1[it, 0, q].astype(F32) + r1[it, 1, q].astype(F32)).astype(BF16)
        start((it, q, "r3", 2), x.at[it, YO, q], r3.at[it, 2, q], yo)

    def rs_three(it, q):
        got(it, q, "r2")
        p, slot, dev = (ZM1, 0, zm) if q % 2 == 0 else (ZP1, 1, zp)
        x[it, p, q] = (base(it, p, q) + r2[it, q].astype(F32)).astype(BF16)
        start((it, q, "r3", slot), x.at[it, p, q], r3.at[it, slot, q], dev)

    def rs_last(it, q):
        s = base(it, OWN, q)
        for i in range(3):
            got(it, q, "r3", i)
            s = s + r3[it, i, q].astype(F32)
        return s * lax.rsqrt(jnp.mean(s * s, axis=-1, keepdims=True) + EPS)

    outs = []

    def post_tile(t):
        at = slice(t * 256, (t + 1) * 256)
        w = e[:, :, :, :, at].reshape(16 * Q * per, 256)
        pout[at, :] = lax.dot_general(
            w, tab[ITERS - 1].reshape(16 * Q * per, width),
            (((0,), (0,)), ((), ())), preferred_element_type=F32,
        ).astype(BF16)
        cp = pltpu.make_async_copy(
            pout.at[pl.ds(t * 256, 256)], post.at[0, pl.ds(t * 256, 256)], lsem.at[parts + Q + t]
        )
        cp.start()
        outs.append(cp)

    for q in range(Q):
        ag_own(0, q, cents.at[0, pl.ds(q * per, per)])

    def unit(j, carry):
        at = pl.ds(pl.multiple_of(j * 32, 32), 32)
        v = pts[at, :].astype(F32)
        n[at, :] = (v * lax.rsqrt(jnp.mean(v * v, axis=-1, keepdims=True) + EPS)).astype(BF16)
        return carry

    for i in range(parts):
        loads[i].wait()
        lax.fori_loop(i * prow // 32, (i + 1) * prow // 32, unit, 0, unroll=2)
    for cp in loads[parts:]:
        cp.wait()

    for it in range(ITERS):
        last = it == ITERS - 1
        if it > 0:
            drain()
        ag_a(it, 0)
        ag_b(it, 0)
        ag_a(it, 1)
        ag_a(it, 2)
        ag_b(it, 1)
        ag_a(it, 3)
        ag_b(it, 2)
        ag_b(it, 3)
        got(it, 0, "s1")
        got(it, 1, "s1")
        logits(it, 0, 3, 0, 2, first=True)
        ag_c(it, 0)
        ag_c(it, 1)
        got(it, 2, "s1")
        got(it, 3, "s1")
        logits(it, 0, 3, 2, 4, 0, 4)
        ag_c(it, 2)
        logits(it, 0, 3, 2, 4, 4, 6)
        ag_c(it, 3)
        ag_d(it, 0)
        ag_d(it, 1)
        ag_e(it, 0)
        for q in range(Q):
            got(it, q, "s0")
            got(it, q, "s2")
        logits(it, 3, 5, 0, 4, 0, 2)
        ag_e(it, 1)
        ag_d(it, 2)
        logits(it, 3, 5, 0, 4, 2, 4)
        ag_e(it, 2)
        ag_d(it, 3)
        logits(it, 3, 5, 0, 4, 4, 6)
        for q in range(2):
            got(it, q, "s3")
            got(it, q, "s4")
        logits(it, 5, 8, 0, 2, 0, 2)
        ag_e(it, 3)
        logits(it, 5, 8, 0, 2, 2, 6)
        for q in range(2, 4):
            got(it, q, "s3")
            got(it, q, "s4")
        logits(it, 5, 8, 2, 4)
        invert()

        def fill(t):
            if last:
                post_tile(t)

        sums(it, 5, 8, 0, 2)
        sums(it, 5, 8, 2, 4)
        rs_one(it, 0)
        rs_one(it, 1)
        sums(it, 3, 5, 0, 4)
        rs_one(it, 2)
        rs_one(it, 3)
        sums(it, 0, 3, 0, 2)
        rs_two(it, 0)
        rs_two(it, 1)
        sums(it, 0, 3, 2, 4)
        rs_two(it, 2)
        rs_early(it, 0)
        rs_early(it, 1)
        rs_y(it, 0)
        rs_two(it, 3)
        rs_y(it, 1)
        rs_early(it, 2)
        rs_early(it, 3)
        fill(0)
        rs_three(it, 0)
        rs_y(it, 2)
        rs_y(it, 3)
        fill(1)
        rs_three(it, 1)
        fill(2)
        rs_three(it, 2)
        fill(3)
        rs_three(it, 3)
        fill(4)
        fill(5)
        for q in range(Q):
            s = rs_last(it, q)
            if last:
                ctr[q] = s
                cp = pltpu.make_async_copy(
                    ctr.at[q], newc.at[0, pl.ds(q * per, per)], lsem.at[parts + q]
                )
                cp.start()
                outs.append(cp)
            else:
                tab[it + 1, OWN, q, 0] = s.astype(BF16)
                ag_own(it + 1, q, tab.at[it + 1, OWN, q, 0])
    drain()
    for cp in outs:
        cp.wait()


def flush(newc_in, post_in, newc, post, sems):
    rows = post.shape[1]
    parts = 4
    cut = rows // parts
    cps = [pltpu.make_async_copy(newc_in, newc, sems.at[parts])]
    for i in range(parts):
        at = pl.ds(i * cut, cut)
        cps.append(pltpu.make_async_copy(post_in.at[0, at], post.at[0, at], sems.at[i]))
    for cp in cps:
        cp.start()
    for cp in cps:
        cp.wait()


def body(points, centroids, tile_counts):
    rows, width = points.shape[1:]
    mine = centroids.shape[1]
    per = mine // Q
    dma = pltpu.SemaphoreType.DMA
    scratch = [
        pltpu.SMEM(tile_counts.shape, jnp.int32),
        pltpu.VMEM((rows, width), BF16),
        pltpu.VMEM((rows, width), BF16),
        pltpu.VMEM((8, Q, 2, per, rows), BF16),
        pltpu.VMEM((8, rows), F32),
        pltpu.VMEM((1, rows), F32),
        pltpu.VMEM((ITERS, 8, Q, 2, per, width), BF16),
        pltpu.VMEM((8, Q, per, width), F32),
        pltpu.VMEM((ITERS, 8, Q, per, width), BF16),
        pltpu.VMEM((ITERS, 8, Q, per, width), BF16),
        pltpu.VMEM((ITERS, 8, Q, per, width), BF16),
        pltpu.VMEM((ITERS, 3, Q, per, width), BF16),
        pltpu.VMEM((ITERS, Q, per, width), BF16),
        pltpu.VMEM((ITERS, 3, Q, per, width), BF16),
        pltpu.VMEM((Q, per, width), F32),
        pltpu.VMEM((rows, width), BF16),
        dma((N_SEMS,)), dma((N_SEMS,)), dma((16,)),
    ]
    anyspace = pl.BlockSpec(memory_space=pl.ANY)
    hbm = pl.BlockSpec(memory_space=pltpu.MemorySpace.HBM)
    shapes = (
        jax.ShapeDtypeStruct((1, mine, width), F32),
        jax.ShapeDtypeStruct((1, rows, width), BF16),
    )
    results = pl.pallas_call(
        kernel,
        out_shape=shapes,
        in_specs=[hbm, hbm, hbm],
        out_specs=(anyspace, anyspace),
        scratch_shapes=scratch,
        compiler_params=pltpu.CompilerParams(
            collective_id=0, has_side_effects=True, vmem_limit_bytes=VLIM * 1024 * 1024
        ),
    )(*[pltpu.with_memory_space_constraint(v, pltpu.MemorySpace.HBM) for v in (tile_counts, points, centroids)])
    return pl.pallas_call(
        flush,
        out_shape=shapes,
        in_specs=[anyspace, anyspace],
        out_specs=(hbm, hbm),
        scratch_shapes=[dma((5,))],
        compiler_params=pltpu.CompilerParams(vmem_limit_bytes=1024 * 1024),
    )(*results)


def solution(mesh):
    return jax.shard_map(
        body,
        mesh=mesh,
        in_specs=(P("grp", "shard", None), P("grp", "shard", None), P()),
        out_specs=(P("grp", "shard", None), P("grp", "shard", None)),
        check_vma=False,
    )
```

```python
import math

import jax
import jax.numpy as jnp
from jax import lax
from jax.experimental import pallas as pl
from jax.experimental.pallas import tpu as pltpu
from jax.sharding import PartitionSpec as P

MESH = pl.DeviceIdType.MESH
TILE = 128
ITERS = 2
EPS = 1e-06
SHARP = 48.0
Q = 4
F32 = jnp.float32
BF16 = jnp.bfloat16
N_SEMS = 224
VLIM = 40
UNROLL = 2
YO, ZP1, ZM1, OWN, ZZ = 0, 1, 2, 3, 4


def kernel(
    counts_in, points, cents, newc, post,
    counts, pts, n, nt, e, den, inv, tab, acc, ssnd, srcv, x, r1, r2, r3, ctr, pout,
    send, recv, lsem,
):
    rows_all, width = n.shape
    per = tab.shape[4]
    g = lax.axis_index("grp")
    sh = lax.axis_index("shard")
    z, y, c = sh // 4, (sh // 2) % 2, sh % 2

    def peer(dz, dy, dc):
        zz = (z + dz) % 4
        yy = (y + dy) % 2
        cc = (c + dc) % 2
        return (g, zz * 4 + yy * 2 + cc)

    zp, zm, yo, sib = peer(1, 0, 0), peer(3, 0, 0), peer(0, 1, 0), peer(0, 0, 1)

    copies = {}
    drained = set()

    def start(key, src, dst, dev):
        i = len(copies)
        cp = pltpu.make_async_remote_copy(
            src_ref=src, dst_ref=dst, send_sem=send.at[i], recv_sem=recv.at[i],
            device_id=dev, device_id_type=MESH,
        )
        cp.start()
        copies[key] = cp

    def got(*key):
        copies[key].wait_recv()

    def drain():
        for key, cp in copies.items():
            if key not in drained:
                cp.wait_send()
                drained.add(key)

    parts = 4
    prow = rows_all // parts
    own_load = []
    for q in range(Q):
        cp = pltpu.make_async_copy(
            cents.at[0, pl.ds(q * per, per)], tab.at[0, OWN, q, 0], lsem.at[parts + q]
        )
        cp.start()
        own_load.append(cp)

    barrier = pltpu.get_barrier_semaphore()
    for dev in (zp, zm, yo, sib):
        pl.semaphore_signal(barrier, inc=1, device_id=dev, device_id_type=MESH)
    loads = []
    for i in range(parts):
        cp = pltpu.make_async_copy(
            points.at[0, pl.ds(i * prow, prow)], pts.at[pl.ds(i * prow, prow)], lsem.at[i]
        )
        cp.start()
        loads.append(cp)
    count_load = pltpu.make_async_copy(counts_in, counts, lsem.at[15])
    count_load.start()
    pl.semaphore_wait(barrier, 4)

    def hop(it, q, name, p, p_dst, dev):
        start((it, q, name), tab.at[it, p, q, 0], tab.at[it, p_dst, q, 0], dev)

    def ag_own(it, q):
        hop(it, q, "y", OWN, YO, yo)
        start((it, q, "s", OWN), tab.at[it, OWN, q, 0], tab.at[it, OWN, q, 1], sib)

    def ag_zp(it, q):
        hop(it, q, "zp", OWN, ZM1, zp)

    def ag_zm(it, q):
        hop(it, q, "zm", OWN, ZP1, zm)

    def share(it, q, p):
        start((it, q, "s", p), tab.at[it, p, q, 0], tab.at[it, p, q, 1], sib)

    def shared(it, pieces):
        for p, q in pieces:
            got(it, q, "s", p)

    def from_zp(it, q):
        got(it, q, "zp")
        if q >= 2:
            hop(it, q, "r6", ZM1, 6, yo)
        if q % 2 == 0:
            hop(it, q, "h", ZM1, ZZ, zp)
        share(it, q, ZM1)

    def from_zm(it, q):
        got(it, q, "zm")
        if q >= 2:
            hop(it, q, "r5", ZP1, 5, yo)
        if q % 2 == 1:
            hop(it, q, "h", ZP1, ZZ, zm)
        share(it, q, ZP1)

    def from_y(it, q):
        got(it, q, "y")
        if q < 2:
            hop(it, q, "r6", YO, 6, zp)
            hop(it, q, "r5", YO, 5, zm)
        share(it, q, YO)

    def from_h(it, q):
        got(it, q, "h")
        if q < 2:
            hop(it, q, "w", ZZ, 7, yo)
        share(it, q, ZZ)

    def from_side(it, q, p):
        got(it, q, "r%d" % p)
        if (q, p) == (2, 6):
            hop(it, q, "w", 6, 7, zp)
        if (q, p) == (3, 5):
            hop(it, q, "w", 5, 7, zm)
        share(it, q, p)

    def from_w(it, q):
        got(it, q, "w")
        share(it, q, 7)

    scale = SHARP / width * math.log2(math.e)
    n_rt = rows_all // 256

    def logits(it, pieces, t0=0, t1=n_rt, first=False):
        m = len(pieces) * 2 * per

        def step(rt, carry):
            at = pl.ds(pl.multiple_of(rt * 256, 256), 256)
            left = [tab[it, p, q].reshape(2 * per, width) for p, q in pieces]
            s = jnp.dot(jnp.concatenate(left, axis=0), nt[:, at], preferred_element_type=F32)
            ex = jnp.exp2(s * scale)
            part = jnp.sum(ex.reshape(m // 8, 8, 256), axis=0)
            den[:, at] = part if first else den[:, at] + part
            ex = ex.astype(BF16).reshape(len(pieces), 2, per, 256)
            for i, (p, q) in enumerate(pieces):
                e[p, q, :, :, at] = ex[i]
            return carry

        lax.fori_loop(t0, t1, step, 0, unroll=UNROLL)

    def invert():
        for t in range(rows_all // TILE):
            at = slice(t * TILE, (t + 1) * TILE)
            live = (t * 16 + sh < counts[g]).astype(F32)
            inv[:, at] = live / jnp.sum(den[:, at], axis=0, keepdims=True)

    def weigh(p0, p1, q0, q1, cores):
        nc = len(range(*cores.indices(2)))
        m = (p1 - p0) * (q1 - q0) * nc * per

        def step(j, carry):
            at = pl.ds(pl.multiple_of(j * 256, 256), 256)
            v = e[p0:p1, q0:q1, cores, :, at].reshape(m, 256).astype(F32) * inv[:, at]
            e[p0:p1, q0:q1, cores, :, at] = v.astype(BF16).reshape(p1 - p0, q1 - q0, nc, per, 256)
            return carry

        lax.fori_loop(0, n_rt, step, 0, unroll=2)

    def send_sums(it, p0, p1, q0, q1):
        for q in range(q0, q1):
            start((it, q, "x", p0), ssnd.at[it, pl.ds(p0, p1 - p0), q], srcv.at[it, pl.ds(p0, p1 - p0), q], sib)

    def sums(it, p0, p1, q0, q1, cores=slice(0, 2)):
        weigh(p0, p1, q0, q1, cores)
        nc = len(range(*cores.indices(2)))
        m = (p1 - p0) * (q1 - q0) * nc * per

        def step(ft, carry):
            at = pl.ds(pl.multiple_of(ft * 256, 256), 256)
            s = jnp.dot(
                e[p0:p1, q0:q1, cores].reshape(m, rows_all), n[:, at], preferred_element_type=F32
            ).reshape(p1 - p0, q1 - q0, nc, per, 256)
            if cores.start == 0:
                acc[p0:p1, q0:q1, :, at] = s[:, :, 0]
            if cores.stop == 2:
                ssnd[it, p0:p1, q0:q1, :, at] = s[:, :, -1].astype(BF16)
            return carry

        lax.fori_loop(0, width // 256, step, 0, unroll=2)
        if cores.stop == 2:
            send_sums(it, p0, p1, q0, q1)

    def base(it, p, q):
        return acc[p, q] + srcv[it, p, q].astype(F32)

    def give(it, q, name, i, p, value, dst, dev):
        x[it, p, q] = value.astype(BF16)
        start((it, q, name, i), x.at[it, p, q], dst, dev)

    def add1(it, q, i):
        got(it, q, "r1", i)
        return r1[it, i, q].astype(F32)

    def rs_seven(it, q):
        got(it, q, "x", 5)
        dev = yo if q < 2 else (zm if q == 2 else zp)
        give(it, q, "r1", 2, 7, base(it, 7, q), r1.at[it, 2, q], dev)

    def rs_rest(it, q):
        if q != 3:
            give(it, q, "r1", 0, 5, base(it, 5, q), r1.at[it, 0, q], zp if q < 2 else yo)
        if q != 2:
            give(it, q, "r1", 1, 6, base(it, 6, q), r1.at[it, 1, q], zm if q < 2 else yo)

    def rs_mid(it, q):
        p, i = (6, 1) if q == 2 else (5, 0)
        give(it, q, "r1", i, p, base(it, p, q) + add1(it, q, 2), r1.at[it, i, q], yo)

    def rs_two(it, q):
        got(it, q, "x", 3)
        v = base(it, ZZ, q)
        if q < 2:
            v = v + add1(it, q, 2)
        give(it, q, "r2", 0, ZZ, v, r2.at[it, q], zm if q % 2 == 0 else zp)

    def to_owner(it, q, p, v):
        slot, dev = (1, zp) if p == ZP1 else (0, zm)
        give(it, q, "r3", slot, p, v, r3.at[it, slot, q], dev)

    def rs_early(it, q):
        got(it, q, "x", 0)
        p = ZP1 if q % 2 == 0 else ZM1
        v = base(it, p, q)
        if q >= 2:
            v = v + add1(it, q, 0 if p == ZP1 else 1)
        to_owner(it, q, p, v)

    def rs_y(it, q):
        v = base(it, YO, q)
        if q < 2:
            v = v + add1(it, q, 0) + add1(it, q, 1)
        give(it, q, "r3", 2, YO, v, r3.at[it, 2, q], yo)

    def rs_three(it, q):
        got(it, q, "r2", 0)
        p = ZM1 if q % 2 == 0 else ZP1
        v = base(it, p, q) + r2[it, q].astype(F32)
        if q >= 2:
            v = v + add1(it, q, 0 if p == ZP1 else 1)
        to_owner(it, q, p, v)

    def rs_last(it, q):
        s = base(it, OWN, q)
        for i in range(3):
            got(it, q, "r3", i)
            s = s + r3[it, i, q].astype(F32)
        return s * lax.rsqrt(jnp.mean(s * s, axis=-1, keepdims=True) + EPS)

    outs = []

    def post_tile(t):
        at = slice(t * 256, (t + 1) * 256)
        w = e[:, :, :, :, at].reshape(16 * Q * per, 256)
        pout[at, :] = lax.dot_general(
            w, tab[ITERS - 1].reshape(16 * Q * per, width),
            (((0,), (0,)), ((), ())), preferred_element_type=F32,
        ).astype(BF16)
        cp = pltpu.make_async_copy(
            pout.at[pl.ds(t * 256, 256)], post.at[0, pl.ds(t * 256, 256)], lsem.at[parts + Q + t]
        )
        cp.start()
        outs.append(cp)

    for cp in own_load:
        cp.wait()
    for i in range(Q):
        ag_zp(0, (0, 2, 3, 1)[i])
        ag_zm(0, (1, 3, 2, 0)[i])
        ag_own(0, i)

    def unit(j, carry):
        at = pl.ds(pl.multiple_of(j * 32, 32), 32)
        v = pts[at, :].astype(F32)
        n[at, :] = (v * lax.rsqrt(jnp.mean(v * v, axis=-1, keepdims=True) + EPS)).astype(BF16)
        return carry

    for i in range(parts):
        loads[i].wait()
        lax.fori_loop(i * prow // 32, (i + 1) * prow // 32, unit, 0, unroll=2)
    count_load.wait()

    def turn(j, carry):
        at = pl.ds(pl.multiple_of(j * 128, 128), 128)
        nt[:, at] = n[at, :].T
        return carry

    lax.fori_loop(0, rows_all // 256, turn, 0)

    for it in range(ITERS):
        last = it == ITERS - 1
        if it > 0:
            drain()
        from_zp(it, 0)
        from_zm(it, 1)
        from_y(it, 0)
        if it == 0:
            lax.fori_loop(rows_all // 256, rows_all // 128, turn, 0)
        from_zp(it, 2)
        from_zm(it, 3)
        from_y(it, 1)
        from_zp(it, 3)
        from_zm(it, 2)
        from_y(it, 2)
        now = [(YO, 0), (YO, 1), (ZM1, 0), (ZM1, 2), (ZP1, 1), (ZP1, 3)]
        shared(it, now)
        logits(it, now, 0, 2, first=True)
        from_zp(it, 1)
        from_zm(it, 0)
        from_y(it, 3)
        logits(it, now, 2, 6, first=True)
        from_h(it, 0)
        from_h(it, 1)
        now = [(YO, 2), (YO, 3), (ZM1, 3), (ZM1, 1), (ZP1, 2), (ZP1, 0)]
        shared(it, now)
        logits(it, now, 0, 2)
        from_side(it, 2, 6)
        from_side(it, 0, 5)
        from_side(it, 0, 6)
        logits(it, now, 2, 6)
        from_side(it, 3, 5)
        from_h(it, 2)
        from_h(it, 3)
        now = [(OWN, 0), (OWN, 1), (OWN, 2), (OWN, 3), (ZZ, 0), (ZZ, 1)]
        shared(it, now)
        logits(it, now, 0, 4)
        from_side(it, 1, 5)
        from_side(it, 1, 6)
        from_side(it, 3, 6)
        logits(it, now, 4, 6)
        now = [(ZZ, 2), (ZZ, 3), (5, 0), (6, 0), (6, 2), (5, 3)]
        shared(it, now)
        logits(it, now, 0, 2)
        from_side(it, 2, 5)
        logits(it, now, 2, 6)
        from_w(it, 0)
        from_w(it, 2)
        now = [(5, 1), (6, 1), (6, 3), (5, 2)]
        shared(it, now)
        logits(it, now, 0, 4)
        from_w(it, 1)
        from_w(it, 3)
        logits(it, now, 4, 6)
        now = [(7, 0), (7, 1), (7, 2), (7, 3)]
        shared(it, now)
        logits(it, now)
        invert()

        def fill(t):
            if last:
                post_tile(t)

        sums(it, 5, 8, 0, 4, slice(1, 2))
        sums(it, 5, 8, 0, 4, slice(0, 1))
        for q in range(Q):
            rs_seven(it, q)
        for q in range(Q):
            rs_rest(it, q)
        sums(it, 3, 5, 0, 4)
        sums(it, 0, 3, 0, 2)
        rs_two(it, 2)
        rs_two(it, 3)
        rs_two(it, 0)
        rs_mid(it, 2)
        sums(it, 0, 3, 2, 4)
        rs_two(it, 1)
        rs_mid(it, 3)
        rs_early(it, 0)
        rs_early(it, 1)
        rs_y(it, 0)
        rs_y(it, 1)
        fill(0)
        rs_early(it, 2)
        rs_early(it, 3)
        rs_y(it, 2)
        rs_y(it, 3)
        rs_three(it, 0)
        fill(1)
        rs_three(it, 1)
        rs_three(it, 2)
        fill(2)
        rs_three(it, 3)
        fill(3)
        if last:
            drain()
        fill(4)
        fill(5)
        for q in range(Q):
            s = rs_last(it, q)
            if last:
                ctr[q] = s
                cp = pltpu.make_async_copy(
                    ctr.at[q], newc.at[0, pl.ds(q * per, per)], lsem.at[parts + q]
                )
                cp.start()
                outs.append(cp)
            else:
                tab[it + 1, OWN, q, 0] = s.astype(BF16)
                ag_zp(it + 1, q)
                ag_zm(it + 1, q)
                ag_own(it + 1, q)
    drain()
    for cp in outs:
        cp.wait()


def flush(newc_in, post_in, newc, post, sems):
    rows = post.shape[1]
    parts = 4
    cut = rows // parts
    cps = [pltpu.make_async_copy(newc_in, newc, sems.at[parts])]
    for i in range(parts):
        at = pl.ds(i * cut, cut)
        cps.append(pltpu.make_async_copy(post_in.at[0, at], post.at[0, at], sems.at[i]))
    for cp in cps:
        cp.start()
    for cp in cps:
        cp.wait()


def body(points, centroids, tile_counts):
    rows, width = points.shape[1:]
    mine = centroids.shape[1]
    per = mine // Q
    dma = pltpu.SemaphoreType.DMA
    scratch = [
        pltpu.SMEM(tile_counts.shape, jnp.int32),
        pltpu.VMEM((rows, width), BF16),
        pltpu.VMEM((rows, width), BF16),
        pltpu.VMEM((width, rows), BF16),
        pltpu.VMEM((8, Q, 2, per, rows), BF16),
        pltpu.VMEM((8, rows), F32),
        pltpu.VMEM((1, rows), F32),
        pltpu.VMEM((ITERS, 8, Q, 2, per, width), BF16),
        pltpu.VMEM((8, Q, per, width), F32),
        pltpu.VMEM((ITERS, 8, Q, per, width), BF16),
        pltpu.VMEM((ITERS, 8, Q, per, width), BF16),
        pltpu.VMEM((ITERS, 8, Q, per, width), BF16),
        pltpu.VMEM((ITERS, 3, Q, per, width), BF16),
        pltpu.VMEM((ITERS, Q, per, width), BF16),
        pltpu.VMEM((ITERS, 3, Q, per, width), BF16),
        pltpu.VMEM((Q, per, width), F32),
        pltpu.VMEM((rows, width), BF16),
        dma((N_SEMS,)), dma((N_SEMS,)), dma((16,)),
    ]
    anyspace = pl.BlockSpec(memory_space=pl.ANY)
    hbm = pl.BlockSpec(memory_space=pltpu.MemorySpace.HBM)
    shapes = (
        jax.ShapeDtypeStruct((1, mine, width), F32),
        jax.ShapeDtypeStruct((1, rows, width), BF16),
    )
    results = pl.pallas_call(
        kernel,
        out_shape=shapes,
        in_specs=[hbm, hbm, hbm],
        out_specs=(anyspace, anyspace),
        scratch_shapes=scratch,
        compiler_params=pltpu.CompilerParams(
            collective_id=0, has_side_effects=True, vmem_limit_bytes=VLIM * 1024 * 1024
        ),
    )(*[pltpu.with_memory_space_constraint(v, pltpu.MemorySpace.HBM) for v in (tile_counts, points, centroids)])
    return pl.pallas_call(
        flush,
        out_shape=shapes,
        in_specs=[anyspace, anyspace],
        out_specs=(hbm, hbm),
        scratch_shapes=[dma((5,))],
        compiler_params=pltpu.CompilerParams(vmem_limit_bytes=1024 * 1024),
    )(*results)


def solution(mesh):
    return jax.shard_map(
        body,
        mesh=mesh,
        in_specs=(P("grp", "shard", None), P("grp", "shard", None), P()),
        out_specs=(P("grp", "shard", None), P("grp", "shard", None)),
        check_vma=False,
    )
```

```python
import math

import jax
import jax.numpy as jnp
from jax import lax
from jax.experimental import pallas as pl
from jax.experimental.pallas import tpu as pltpu
from jax.sharding import PartitionSpec as P

MESH = pl.DeviceIdType.MESH
TILE = 128
ITERS = 2
EPS = 1e-06
SHARP = 48.0
Q = 4
F32 = jnp.float32
BF16 = jnp.bfloat16
N_SEMS = 224
VLIM = 40
UNROLL = 2
YO, ZP1, ZM1, OWN, ZZ = 0, 1, 2, 3, 4


def kernel(
    counts_in, points, cents, newc, post,
    counts, pts, n, nt, e, den, inv, tab, acc, ssnd, srcv, x, r1, r2, r3, ctr, pout,
    send, recv, lsem,
):
    rows_all, width = n.shape
    per = tab.shape[4]
    g = lax.axis_index("grp")
    sh = lax.axis_index("shard")
    z, y, c = sh // 4, (sh // 2) % 2, sh % 2

    def peer(dz, dy, dc):
        zz = (z + dz) % 4
        yy = (y + dy) % 2
        cc = (c + dc) % 2
        return (g, zz * 4 + yy * 2 + cc)

    zp, zm, yo, sib = peer(1, 0, 0), peer(3, 0, 0), peer(0, 1, 0), peer(0, 0, 1)

    copies = {}
    drained = set()

    def start(key, src, dst, dev):
        i = len(copies)
        cp = pltpu.make_async_remote_copy(
            src_ref=src, dst_ref=dst, send_sem=send.at[i], recv_sem=recv.at[i],
            device_id=dev, device_id_type=MESH,
        )
        cp.start()
        copies[key] = cp

    def got(*key):
        copies[key].wait_recv()

    def drain():
        for key, cp in copies.items():
            if key not in drained:
                cp.wait_send()
                drained.add(key)

    parts = 4
    prow = rows_all // parts
    own_load = []
    for q in range(Q):
        cp = pltpu.make_async_copy(
            cents.at[0, pl.ds(q * per, per)], tab.at[0, OWN, q, 0], lsem.at[parts + q]
        )
        cp.start()
        own_load.append(cp)

    barrier = pltpu.get_barrier_semaphore()
    for dev in (zp, zm, yo, sib):
        pl.semaphore_signal(barrier, inc=1, device_id=dev, device_id_type=MESH)
    loads = []
    for i in range(parts):
        cp = pltpu.make_async_copy(
            points.at[0, pl.ds(i * prow, prow)], pts.at[pl.ds(i * prow, prow)], lsem.at[i]
        )
        cp.start()
        loads.append(cp)
    count_load = pltpu.make_async_copy(counts_in, counts, lsem.at[15])
    count_load.start()
    pl.semaphore_wait(barrier, 4)

    def hop(it, q, name, p, p_dst, dev):
        start((it, q, name), tab.at[it, p, q, 0], tab.at[it, p_dst, q, 0], dev)

    def ag_own(it, q):
        hop(it, q, "y", OWN, YO, yo)
        start((it, q, "s", OWN), tab.at[it, OWN, q, 0], tab.at[it, OWN, q, 1], sib)

    def ag_zp(it, q):
        hop(it, q, "zp", OWN, ZM1, zp)

    def ag_zm(it, q):
        hop(it, q, "zm", OWN, ZP1, zm)

    def share(it, q, p):
        start((it, q, "s", p), tab.at[it, p, q, 0], tab.at[it, p, q, 1], sib)

    def shared(it, pieces):
        for p, q in pieces:
            got(it, q, "s", p)

    def from_zp(it, q):
        got(it, q, "zp")
        if q >= 2:
            hop(it, q, "r6", ZM1, 6, yo)
        if q % 2 == 0:
            hop(it, q, "h", ZM1, ZZ, zp)
        share(it, q, ZM1)

    def from_zm(it, q):
        got(it, q, "zm")
        if q >= 2:
            hop(it, q, "r5", ZP1, 5, yo)
        if q % 2 == 1:
            hop(it, q, "h", ZP1, ZZ, zm)
        share(it, q, ZP1)

    def from_y(it, q):
        got(it, q, "y")
        if q < 2:
            hop(it, q, "r6", YO, 6, zp)
            hop(it, q, "r5", YO, 5, zm)
        share(it, q, YO)

    def from_h(it, q):
        got(it, q, "h")
        if q < 2:
            hop(it, q, "w", ZZ, 7, yo)
        share(it, q, ZZ)

    def from_side(it, q, p):
        got(it, q, "r%d" % p)
        if (q, p) == (2, 6):
            hop(it, q, "w", 6, 7, zp)
        if (q, p) == (3, 5):
            hop(it, q, "w", 5, 7, zm)
        share(it, q, p)

    def from_w(it, q):
        got(it, q, "w")
        share(it, q, 7)

    scale = SHARP / width * math.log2(math.e)
    n_rt = rows_all // 256

    def logits(it, pieces, t0=0, t1=n_rt, first=False):
        m = len(pieces) * 2 * per

        def step(rt, carry):
            at = pl.ds(pl.multiple_of(rt * 256, 256), 256)
            left = [tab[it, p, q].reshape(2 * per, width) for p, q in pieces]
            s = jnp.dot(jnp.concatenate(left, axis=0), nt[:, at], preferred_element_type=F32)
            ex = jnp.exp2(s * scale)
            part = jnp.sum(ex.reshape(m // 8, 8, 256), axis=0)
            den[:, at] = part if first else den[:, at] + part
            ex = ex.astype(BF16).reshape(len(pieces), 2, per, 256)
            for i, (p, q) in enumerate(pieces):
                e[p, q, :, :, at] = ex[i]
            return carry

        lax.fori_loop(t0, t1, step, 0, unroll=UNROLL)

    def invert():
        for t in range(rows_all // TILE):
            at = slice(t * TILE, (t + 1) * TILE)
            live = (t * 16 + sh < counts[g]).astype(F32)
            inv[:, at] = live / jnp.sum(den[:, at], axis=0, keepdims=True)

    def weigh(p0, p1, q0, q1):
        m = (p1 - p0) * (q1 - q0) * 2 * per

        def step(j, carry):
            at = pl.ds(pl.multiple_of(j * 256, 256), 256)
            v = e[p0:p1, q0:q1, :, :, at].reshape(m, 256).astype(F32) * inv[:, at]
            e[p0:p1, q0:q1, :, :, at] = v.astype(BF16).reshape(p1 - p0, q1 - q0, 2, per, 256)
            return carry

        lax.fori_loop(0, n_rt, step, 0, unroll=2)

    n_ft = width // 256

    def sums(it, p0, p1, q0, q1, f0=0, f1=n_ft):
        m = (p1 - p0) * (q1 - q0) * 2 * per
        if f0 == 0:
            weigh(p0, p1, q0, q1)

        def step(ft, carry):
            at = pl.ds(pl.multiple_of(ft * 256, 256), 256)
            s = jnp.dot(
                e[p0:p1, q0:q1].reshape(m, rows_all), n[:, at], preferred_element_type=F32
            ).reshape(p1 - p0, q1 - q0, 2, per, 256)
            acc[p0:p1, q0:q1, :, at] = s[:, :, 0]
            ssnd[it, p0:p1, q0:q1, :, at] = s[:, :, 1].astype(BF16)
            return carry

        lax.fori_loop(f0, f1, step, 0, unroll=2)
        if f1 == n_ft:
            for q in range(q0, q1):
                start((it, q, "x", p0), ssnd.at[it, pl.ds(p0, p1 - p0), q], srcv.at[it, pl.ds(p0, p1 - p0), q], sib)

    def base(it, p, q):
        return acc[p, q] + srcv[it, p, q].astype(F32)

    def give(it, q, name, i, p, value, dst, dev):
        x[it, p, q] = value.astype(BF16)
        start((it, q, name, i), x.at[it, p, q], dst, dev)

    def add1(it, q, i):
        got(it, q, "r1", i)
        return r1[it, i, q].astype(F32)

    def rs_seven(it, q):
        got(it, q, "x", 7)
        dev = yo if q < 2 else (zm if q == 2 else zp)
        give(it, q, "r1", 2, 7, base(it, 7, q), r1.at[it, 2, q], dev)

    def rs_rest(it, q):
        got(it, q, "x", 5)
        if q != 3:
            give(it, q, "r1", 0, 5, base(it, 5, q), r1.at[it, 0, q], zp if q < 2 else yo)
        if q != 2:
            give(it, q, "r1", 1, 6, base(it, 6, q), r1.at[it, 1, q], zm if q < 2 else yo)

    def rs_mid(it, q):
        p, i = (6, 1) if q == 2 else (5, 0)
        give(it, q, "r1", i, p, base(it, p, q) + add1(it, q, 2), r1.at[it, i, q], yo)

    def rs_two(it, q):
        got(it, q, "x", 3)
        v = base(it, ZZ, q)
        if q < 2:
            v = v + add1(it, q, 2)
        give(it, q, "r2", 0, ZZ, v, r2.at[it, q], zm if q % 2 == 0 else zp)

    def to_owner(it, q, p, v):
        slot, dev = (1, zp) if p == ZP1 else (0, zm)
        give(it, q, "r3", slot, p, v, r3.at[it, slot, q], dev)

    def rs_early(it, q):
        got(it, q, "x", 0)
        p = ZP1 if q % 2 == 0 else ZM1
        v = base(it, p, q)
        if q >= 2:
            v = v + add1(it, q, 0 if p == ZP1 else 1)
        to_owner(it, q, p, v)

    def rs_y(it, q):
        v = base(it, YO, q)
        if q < 2:
            v = v + add1(it, q, 0) + add1(it, q, 1)
        give(it, q, "r3", 2, YO, v, r3.at[it, 2, q], yo)

    def rs_three(it, q):
        got(it, q, "r2", 0)
        p = ZM1 if q % 2 == 0 else ZP1
        v = base(it, p, q) + r2[it, q].astype(F32)
        if q >= 2:
            v = v + add1(it, q, 0 if p == ZP1 else 1)
        to_owner(it, q, p, v)

    def rs_last(it, q):
        s = base(it, OWN, q)
        for i in range(3):
            got(it, q, "r3", i)
            s = s + r3[it, i, q].astype(F32)
        return s * lax.rsqrt(jnp.mean(s * s, axis=-1, keepdims=True) + EPS)

    outs = []

    def post_tile(t):
        at = slice(t * 256, (t + 1) * 256)
        w = e[:, :, :, :, at].reshape(16 * Q * per, 256)
        pout[at, :] = lax.dot_general(
            w, tab[ITERS - 1].reshape(16 * Q * per, width),
            (((0,), (0,)), ((), ())), preferred_element_type=F32,
        ).astype(BF16)
        cp = pltpu.make_async_copy(
            pout.at[pl.ds(t * 256, 256)], post.at[0, pl.ds(t * 256, 256)], lsem.at[parts + Q + t]
        )
        cp.start()
        outs.append(cp)

    for cp in own_load:
        cp.wait()
    for i in range(Q):
        ag_zp(0, (0, 2, 3, 1)[i])
        ag_zm(0, (1, 3, 2, 0)[i])
        ag_own(0, i)

    def unit(j, carry):
        at = pl.ds(pl.multiple_of(j * 32, 32), 32)
        v = pts[at, :].astype(F32)
        n[at, :] = (v * lax.rsqrt(jnp.mean(v * v, axis=-1, keepdims=True) + EPS)).astype(BF16)
        return carry

    for i in range(parts):
        loads[i].wait()
        lax.fori_loop(i * prow // 32, (i + 1) * prow // 32, unit, 0, unroll=2)
    count_load.wait()

    def turn(j, carry):
        at = pl.ds(pl.multiple_of(j * 128, 128), 128)
        nt[:, at] = n[at, :].T
        return carry

    lax.fori_loop(0, rows_all // 256, turn, 0)

    for it in range(ITERS):
        last = it == ITERS - 1
        if it > 0:
            drain()
        from_zp(it, 0)
        from_zm(it, 1)
        from_y(it, 0)
        if it == 0:
            lax.fori_loop(rows_all // 256, rows_all // 128, turn, 0)
        from_zp(it, 2)
        from_zm(it, 3)
        from_y(it, 1)
        from_zp(it, 3)
        from_zm(it, 2)
        from_y(it, 2)
        now = [(YO, 0), (YO, 1), (ZM1, 0), (ZM1, 2), (ZP1, 1), (ZP1, 3)]
        shared(it, now)
        logits(it, now, 0, 2, first=True)
        from_zp(it, 1)
        from_zm(it, 0)
        from_y(it, 3)
        logits(it, now, 2, 6, first=True)
        from_h(it, 0)
        from_h(it, 1)
        now = [(YO, 2), (YO, 3), (ZM1, 3), (ZM1, 1), (ZP1, 2), (ZP1, 0)]
        shared(it, now)
        logits(it, now, 0, 2)
        from_side(it, 2, 6)
        from_side(it, 0, 5)
        from_side(it, 0, 6)
        logits(it, now, 2, 6)
        from_side(it, 3, 5)
        from_h(it, 2)
        from_h(it, 3)
        now = [(OWN, 0), (OWN, 1), (OWN, 2), (OWN, 3), (ZZ, 0), (ZZ, 1)]
        shared(it, now)
        logits(it, now, 0, 4)
        from_side(it, 1, 5)
        from_side(it, 1, 6)
        from_side(it, 3, 6)
        logits(it, now, 4, 6)
        now = [(ZZ, 2), (ZZ, 3), (5, 0), (6, 0), (6, 2), (5, 3)]
        shared(it, now)
        logits(it, now, 0, 2)
        from_side(it, 2, 5)
        logits(it, now, 2, 6)
        from_w(it, 0)
        from_w(it, 2)
        now = [(5, 1), (6, 1), (6, 3), (5, 2)]
        shared(it, now)
        logits(it, now, 0, 4)
        from_w(it, 1)
        from_w(it, 3)
        logits(it, now, 4, 6)
        now = [(7, 0), (7, 1), (7, 2), (7, 3)]
        shared(it, now)
        logits(it, now)
        invert()

        def fill(t):
            if last:
                post_tile(t)

        sums(it, 7, 8, 0, 4)
        sums(it, 5, 7, 0, 4)
        for q in (2, 3, 0, 1):
            rs_seven(it, q)
        sums(it, 3, 5, 0, 4)
        for q in range(Q):
            rs_rest(it, q)
        sums(it, 0, 3, 0, 2)
        rs_two(it, 2)
        rs_two(it, 3)
        sums(it, 0, 3, 2, 4, 0, 2)
        rs_two(it, 0)
        rs_mid(it, 2)
        sums(it, 0, 3, 2, 4, 2, 4)
        rs_two(it, 1)
        rs_mid(it, 3)
        rs_early(it, 0)
        rs_early(it, 1)
        fill(0)
        rs_y(it, 0)
        rs_y(it, 1)
        rs_early(it, 2)
        rs_early(it, 3)
        rs_y(it, 2)
        rs_y(it, 3)
        fill(1)
        rs_three(it, 0)
        rs_three(it, 2)
        fill(2)
        rs_three(it, 1)
        rs_three(it, 3)
        fill(3)
        if last:
            drain()
        fill(4)
        fill(5)
        for q in range(Q):
            s = rs_last(it, q)
            if last:
                ctr[q] = s
                cp = pltpu.make_async_copy(
                    ctr.at[q], newc.at[0, pl.ds(q * per, per)], lsem.at[parts + q]
                )
                cp.start()
                outs.append(cp)
            else:
                tab[it + 1, OWN, q, 0] = s.astype(BF16)
                ag_zp(it + 1, q)
                ag_zm(it + 1, q)
                ag_own(it + 1, q)
    drain()
    for cp in outs:
        cp.wait()


def flush(newc_in, post_in, newc, post, sems):
    rows = post.shape[1]
    parts = 4
    cut = rows // parts
    cps = [pltpu.make_async_copy(newc_in, newc, sems.at[parts])]
    for i in range(parts):
        at = pl.ds(i * cut, cut)
        cps.append(pltpu.make_async_copy(post_in.at[0, at], post.at[0, at], sems.at[i]))
    for cp in cps:
        cp.start()
    for cp in cps:
        cp.wait()


def body(points, centroids, tile_counts):
    rows, width = points.shape[1:]
    mine = centroids.shape[1]
    per = mine // Q
    dma = pltpu.SemaphoreType.DMA
    scratch = [
        pltpu.SMEM(tile_counts.shape, jnp.int32),
        pltpu.VMEM((rows, width), BF16),
        pltpu.VMEM((rows, width), BF16),
        pltpu.VMEM((width, rows), BF16),
        pltpu.VMEM((8, Q, 2, per, rows), BF16),
        pltpu.VMEM((8, rows), F32),
        pltpu.VMEM((1, rows), F32),
        pltpu.VMEM((ITERS, 8, Q, 2, per, width), BF16),
        pltpu.VMEM((8, Q, per, width), F32),
        pltpu.VMEM((ITERS, 8, Q, per, width), BF16),
        pltpu.VMEM((ITERS, 8, Q, per, width), BF16),
        pltpu.VMEM((ITERS, 8, Q, per, width), BF16),
        pltpu.VMEM((ITERS, 3, Q, per, width), BF16),
        pltpu.VMEM((ITERS, Q, per, width), BF16),
        pltpu.VMEM((ITERS, 3, Q, per, width), BF16),
        pltpu.VMEM((Q, per, width), F32),
        pltpu.VMEM((rows, width), BF16),
        dma((N_SEMS,)), dma((N_SEMS,)), dma((16,)),
    ]
    anyspace = pl.BlockSpec(memory_space=pl.ANY)
    hbm = pl.BlockSpec(memory_space=pltpu.MemorySpace.HBM)
    shapes = (
        jax.ShapeDtypeStruct((1, mine, width), F32),
        jax.ShapeDtypeStruct((1, rows, width), BF16),
    )
    results = pl.pallas_call(
        kernel,
        out_shape=shapes,
        in_specs=[hbm, hbm, hbm],
        out_specs=(anyspace, anyspace),
        scratch_shapes=scratch,
        compiler_params=pltpu.CompilerParams(
            collective_id=0, has_side_effects=True, vmem_limit_bytes=VLIM * 1024 * 1024
        ),
    )(*[pltpu.with_memory_space_constraint(v, pltpu.MemorySpace.HBM) for v in (tile_counts, points, centroids)])
    return pl.pallas_call(
        flush,
        out_shape=shapes,
        in_specs=[anyspace, anyspace],
        out_specs=(hbm, hbm),
        scratch_shapes=[dma((5,))],
        compiler_params=pltpu.CompilerParams(vmem_limit_bytes=1024 * 1024),
    )(*results)


def solution(mesh):
    return jax.shard_map(
        body,
        mesh=mesh,
        in_specs=(P("grp", "shard", None), P("grp", "shard", None), P()),
        out_specs=(P("grp", "shard", None), P("grp", "shard", None)),
        check_vma=False,
    )
```

```python
import math

import jax
import jax.numpy as jnp
from jax import lax
from jax.experimental import pallas as pl
from jax.experimental.pallas import tpu as pltpu
from jax.sharding import PartitionSpec as P

MESH = pl.DeviceIdType.MESH
TILE = 128
ITERS = 2
EPS = 1e-06
SHARP = 48.0
Q = 4
F32 = jnp.float32
BF16 = jnp.bfloat16
N_SEMS = 224
VLIM = 40
UNROLL = 2
YO, ZP1, ZM1, OWN, ZZ = 0, 1, 2, 3, 4


def kernel(
    counts_in, points, cents, newc, post,
    counts, pts, n, nt, e, den, inv, tab, acc, ssnd, srcv, x, r1, r2, r3, ctr, pout,
    send, recv, lsem,
):
    rows_all, width = n.shape
    per = tab.shape[4]
    g = lax.axis_index("grp")
    sh = lax.axis_index("shard")
    z, y, c = sh // 4, (sh // 2) % 2, sh % 2

    def peer(dz, dy, dc):
        zz = (z + dz) % 4
        yy = (y + dy) % 2
        cc = (c + dc) % 2
        return (g, zz * 4 + yy * 2 + cc)

    zp, zm, yo, sib = peer(1, 0, 0), peer(3, 0, 0), peer(0, 1, 0), peer(0, 0, 1)

    copies = {}
    drained = set()

    def start(key, src, dst, dev):
        i = len(copies)
        cp = pltpu.make_async_remote_copy(
            src_ref=src, dst_ref=dst, send_sem=send.at[i], recv_sem=recv.at[i],
            device_id=dev, device_id_type=MESH,
        )
        cp.start()
        copies[key] = cp

    def got(*key):
        copies[key].wait_recv()

    def drain():
        for key, cp in copies.items():
            if key not in drained:
                cp.wait_send()
                drained.add(key)

    parts = 4
    prow = rows_all // parts
    own_load = []
    for q in range(Q):
        cp = pltpu.make_async_copy(
            cents.at[0, pl.ds(q * per, per)], tab.at[0, OWN, q, 0], lsem.at[parts + q]
        )
        cp.start()
        own_load.append(cp)

    barrier = pltpu.get_barrier_semaphore()
    for dev in (zp, zm, yo, sib):
        pl.semaphore_signal(barrier, inc=1, device_id=dev, device_id_type=MESH)
    loads = []
    for i in range(parts):
        cp = pltpu.make_async_copy(
            points.at[0, pl.ds(i * prow, prow)], pts.at[pl.ds(i * prow, prow)], lsem.at[i]
        )
        cp.start()
        loads.append(cp)
    count_load = pltpu.make_async_copy(counts_in, counts, lsem.at[15])
    count_load.start()
    pl.semaphore_wait(barrier, 4)

    def hop(it, q, name, p, p_dst, dev):
        start((it, q, name), tab.at[it, p, q, 0], tab.at[it, p_dst, q, 0], dev)

    def ag_own(it, q):
        hop(it, q, "y", OWN, YO, yo)
        start((it, q, "s", OWN), tab.at[it, OWN, q, 0], tab.at[it, OWN, q, 1], sib)

    def ag_zp(it, q):
        hop(it, q, "zp", OWN, ZM1, zp)

    def ag_zm(it, q):
        hop(it, q, "zm", OWN, ZP1, zm)

    def share(it, q, p):
        start((it, q, "s", p), tab.at[it, p, q, 0], tab.at[it, p, q, 1], sib)

    def shared(it, pieces):
        for p, q in pieces:
            got(it, q, "s", p)

    def from_zp(it, q):
        got(it, q, "zp")
        if q >= 2:
            hop(it, q, "r6", ZM1, 6, yo)
        if q % 2 == 0:
            hop(it, q, "h", ZM1, ZZ, zp)
        share(it, q, ZM1)

    def from_zm(it, q):
        got(it, q, "zm")
        if q >= 2:
            hop(it, q, "r5", ZP1, 5, yo)
        if q % 2 == 1:
            hop(it, q, "h", ZP1, ZZ, zm)
        share(it, q, ZP1)

    def from_y(it, q):
        got(it, q, "y")
        if q < 2:
            hop(it, q, "r6", YO, 6, zp)
            hop(it, q, "r5", YO, 5, zm)
        share(it, q, YO)

    def from_h(it, q):
        got(it, q, "h")
        if q < 2:
            hop(it, q, "w", ZZ, 7, yo)
        share(it, q, ZZ)

    def from_side(it, q, p):
        got(it, q, "r%d" % p)
        if (q, p) == (2, 6):
            hop(it, q, "w", 6, 7, zp)
        if (q, p) == (3, 5):
            hop(it, q, "w", 5, 7, zm)
        share(it, q, p)

    def from_w(it, q):
        got(it, q, "w")
        share(it, q, 7)

    scale = SHARP / width * math.log2(math.e)
    n_rt = rows_all // 256

    def logits(it, pieces, t0=0, t1=n_rt, first=False):
        m = len(pieces) * 2 * per

        def step(rt, carry):
            at = pl.ds(pl.multiple_of(rt * 256, 256), 256)
            left = [tab[it, p, q].reshape(2 * per, width) for p, q in pieces]
            s = jnp.dot(jnp.concatenate(left, axis=0), nt[:, at], preferred_element_type=F32)
            ex = jnp.exp2(s * scale)
            part = jnp.sum(ex.reshape(m // 8, 8, 256), axis=0)
            den[:, at] = part if first else den[:, at] + part
            ex = ex.astype(BF16).reshape(len(pieces), 2, per, 256)
            for i, (p, q) in enumerate(pieces):
                e[p, q, :, :, at] = ex[i]
            return carry

        lax.fori_loop(t0, t1, step, 0, unroll=UNROLL)

    def invert():
        for t in range(rows_all // TILE):
            at = slice(t * TILE, (t + 1) * TILE)
            live = (t * 16 + sh < counts[g]).astype(F32)
            inv[:, at] = live / jnp.sum(den[:, at], axis=0, keepdims=True)

    def weigh(p0, p1, q0, q1):
        m = (p1 - p0) * (q1 - q0) * 2 * per

        def step(j, carry):
            at = pl.ds(pl.multiple_of(j * 256, 256), 256)
            v = e[p0:p1, q0:q1, :, :, at].reshape(m, 256) * inv[:, at].astype(BF16)
            e[p0:p1, q0:q1, :, :, at] = v.astype(BF16).reshape(p1 - p0, q1 - q0, 2, per, 256)
            return carry

        lax.fori_loop(0, n_rt, step, 0, unroll=2)

    n_ft = width // 256

    def sums(it, p0, p1, q0, q1, f0=0, f1=n_ft):
        m = (p1 - p0) * (q1 - q0) * 2 * per
        if f0 == 0:
            weigh(p0, p1, q0, q1)

        def step(ft, carry):
            at = pl.ds(pl.multiple_of(ft * 256, 256), 256)
            s = jnp.dot(
                e[p0:p1, q0:q1].reshape(m, rows_all), n[:, at], preferred_element_type=F32
            ).reshape(p1 - p0, q1 - q0, 2, per, 256)
            acc[p0:p1, q0:q1, :, at] = s[:, :, 0]
            ssnd[it, p0:p1, q0:q1, :, at] = s[:, :, 1].astype(BF16)
            return carry

        lax.fori_loop(f0, f1, step, 0, unroll=2)
        if f1 == n_ft:
            for q in range(q0, q1):
                start((it, q, "x", p0), ssnd.at[it, pl.ds(p0, p1 - p0), q], srcv.at[it, pl.ds(p0, p1 - p0), q], sib)

    def base(it, p, q):
        return acc[p, q] + srcv[it, p, q].astype(F32)

    def give(it, q, name, i, p, value, dst, dev):
        x[it, p, q] = value.astype(BF16)
        start((it, q, name, i), x.at[it, p, q], dst, dev)

    def add1(it, q, i):
        got(it, q, "r1", i)
        return r1[it, i, q].astype(F32)

    def rs_seven(it, q):
        got(it, q, "x", 7)
        dev = yo if q < 2 else (zm if q == 2 else zp)
        give(it, q, "r1", 2, 7, base(it, 7, q), r1.at[it, 2, q], dev)

    def rs_rest(it, q):
        got(it, q, "x", 5)
        if q != 3:
            give(it, q, "r1", 0, 5, base(it, 5, q), r1.at[it, 0, q], zp if q < 2 else yo)
        if q != 2:
            give(it, q, "r1", 1, 6, base(it, 6, q), r1.at[it, 1, q], zm if q < 2 else yo)

    def rs_mid(it, q):
        p, i = (6, 1) if q == 2 else (5, 0)
        give(it, q, "r1", i, p, base(it, p, q) + add1(it, q, 2), r1.at[it, i, q], yo)

    def rs_two(it, q):
        got(it, q, "x", 3)
        v = base(it, ZZ, q)
        if q < 2:
            v = v + add1(it, q, 2)
        give(it, q, "r2", 0, ZZ, v, r2.at[it, q], zm if q % 2 == 0 else zp)

    def to_owner(it, q, p, v):
        slot, dev = (1, zp) if p == ZP1 else (0, zm)
        give(it, q, "r3", slot, p, v, r3.at[it, slot, q], dev)

    def rs_early(it, q):
        got(it, q, "x", 0)
        p = ZP1 if q % 2 == 0 else ZM1
        v = base(it, p, q)
        if q >= 2:
            v = v + add1(it, q, 0 if p == ZP1 else 1)
        to_owner(it, q, p, v)

    def rs_y(it, q):
        v = base(it, YO, q)
        if q < 2:
            v = v + add1(it, q, 0) + add1(it, q, 1)
        give(it, q, "r3", 2, YO, v, r3.at[it, 2, q], yo)

    def rs_three(it, q):
        got(it, q, "r2", 0)
        p = ZM1 if q % 2 == 0 else ZP1
        v = base(it, p, q) + r2[it, q].astype(F32)
        if q >= 2:
            v = v + add1(it, q, 0 if p == ZP1 else 1)
        to_owner(it, q, p, v)

    def rs_last(it, q):
        s = base(it, OWN, q)
        for i in range(3):
            got(it, q, "r3", i)
            s = s + r3[it, i, q].astype(F32)
        return s * lax.rsqrt(jnp.mean(s * s, axis=-1, keepdims=True) + EPS)

    outs = []

    def post_tile(t):
        at = slice(t * 256, (t + 1) * 256)
        w = e[:, :, :, :, at].reshape(16 * Q * per, 256)
        pout[at, :] = lax.dot_general(
            w, tab[ITERS - 1].reshape(16 * Q * per, width),
            (((0,), (0,)), ((), ())), preferred_element_type=F32,
        ).astype(BF16)
        cp = pltpu.make_async_copy(
            pout.at[pl.ds(t * 256, 256)], post.at[0, pl.ds(t * 256, 256)], lsem.at[parts + Q + t]
        )
        cp.start()
        outs.append(cp)

    for cp in own_load:
        cp.wait()
    for i in range(Q):
        ag_zp(0, (0, 2, 3, 1)[i])
        ag_zm(0, (1, 3, 2, 0)[i])
        ag_own(0, i)

    def unit(j, carry):
        at = pl.ds(pl.multiple_of(j * 32, 32), 32)
        v = pts[at, :].astype(F32)
        n[at, :] = (v * lax.rsqrt(jnp.mean(v * v, axis=-1, keepdims=True) + EPS)).astype(BF16)
        return carry

    for i in range(parts):
        loads[i].wait()
        lax.fori_loop(i * prow // 32, (i + 1) * prow // 32, unit, 0, unroll=2)
    count_load.wait()

    def turn(j, carry):
        at = pl.ds(pl.multiple_of(j * 128, 128), 128)
        nt[:, at] = n[at, :].T
        return carry

    lax.fori_loop(0, rows_all // 256, turn, 0)

    for it in range(ITERS):
        last = it == ITERS - 1
        if it > 0:
            drain()
        from_zp(it, 0)
        from_zm(it, 1)
        from_y(it, 0)
        if it == 0:
            lax.fori_loop(rows_all // 256, rows_all // 128, turn, 0)
        from_zp(it, 2)
        from_zm(it, 3)
        from_y(it, 1)
        from_zp(it, 3)
        from_zm(it, 2)
        from_y(it, 2)
        now = [(YO, 0), (YO, 1), (ZM1, 0), (ZM1, 2), (ZP1, 1), (ZP1, 3)]
        shared(it, now)
        logits(it, now, 0, 2, first=True)
        from_zp(it, 1)
        from_zm(it, 0)
        from_y(it, 3)
        logits(it, now, 2, 6, first=True)
        from_h(it, 0)
        from_h(it, 1)
        now = [(YO, 2), (YO, 3), (ZM1, 3), (ZM1, 1), (ZP1, 2), (ZP1, 0)]
        shared(it, now)
        logits(it, now, 0, 2)
        from_side(it, 2, 6)
        from_side(it, 0, 5)
        from_side(it, 0, 6)
        logits(it, now, 2, 6)
        from_side(it, 3, 5)
        from_h(it, 2)
        from_h(it, 3)
        now = [(OWN, 0), (OWN, 1), (OWN, 2), (OWN, 3), (ZZ, 0), (ZZ, 1)]
        shared(it, now)
        logits(it, now, 0, 4)
        from_side(it, 1, 5)
        from_side(it, 1, 6)
        from_side(it, 3, 6)
        logits(it, now, 4, 6)
        now = [(ZZ, 2), (ZZ, 3), (5, 0), (6, 0), (6, 2), (5, 3)]
        shared(it, now)
        logits(it, now, 0, 2)
        from_side(it, 2, 5)
        logits(it, now, 2, 6)
        from_w(it, 0)
        from_w(it, 2)
        now = [(5, 1), (6, 1), (6, 3), (5, 2)]
        shared(it, now)
        logits(it, now, 0, 4)
        from_w(it, 1)
        from_w(it, 3)
        logits(it, now, 4, 6)
        now = [(7, 0), (7, 1), (7, 2), (7, 3)]
        shared(it, now)
        logits(it, now)
        invert()

        def fill(t):
            if last:
                post_tile(t)

        sums(it, 7, 8, 0, 4)
        sums(it, 5, 7, 0, 4)
        for q in (2, 3, 0, 1):
            rs_seven(it, q)
        sums(it, 3, 5, 0, 4)
        for q in range(Q):
            rs_rest(it, q)
        sums(it, 0, 3, 0, 2)
        rs_two(it, 2)
        rs_two(it, 3)
        sums(it, 0, 3, 2, 4, 0, 2)
        rs_two(it, 0)
        rs_mid(it, 2)
        sums(it, 0, 3, 2, 4, 2, 4)
        rs_two(it, 1)
        rs_mid(it, 3)
        rs_early(it, 0)
        rs_early(it, 1)
        fill(0)
        rs_y(it, 0)
        rs_y(it, 1)
        rs_early(it, 2)
        rs_early(it, 3)
        rs_y(it, 2)
        rs_y(it, 3)
        fill(1)
        rs_three(it, 0)
        rs_three(it, 2)
        fill(2)
        rs_three(it, 1)
        rs_three(it, 3)
        fill(3)
        if last:
            drain()
        fill(4)
        fill(5)
        for q in (0, 2, 1, 3):
            s = rs_last(it, q)
            if last:
                ctr[q] = s
                cp = pltpu.make_async_copy(
                    ctr.at[q], newc.at[0, pl.ds(q * per, per)], lsem.at[parts + q]
                )
                cp.start()
                outs.append(cp)
            else:
                tab[it + 1, OWN, q, 0] = s.astype(BF16)
                ag_zp(it + 1, q)
                ag_zm(it + 1, q)
                ag_own(it + 1, q)
    drain()
    for cp in outs:
        cp.wait()


def flush(newc_in, post_in, newc, post, sems):
    rows = post.shape[1]
    parts = 4
    cut = rows // parts
    cps = [pltpu.make_async_copy(newc_in, newc, sems.at[parts])]
    for i in range(parts):
        at = pl.ds(i * cut, cut)
        cps.append(pltpu.make_async_copy(post_in.at[0, at], post.at[0, at], sems.at[i]))
    for cp in cps:
        cp.start()
    for cp in cps:
        cp.wait()


def body(points, centroids, tile_counts):
    rows, width = points.shape[1:]
    mine = centroids.shape[1]
    per = mine // Q
    dma = pltpu.SemaphoreType.DMA
    scratch = [
        pltpu.SMEM(tile_counts.shape, jnp.int32),
        pltpu.VMEM((rows, width), BF16),
        pltpu.VMEM((rows, width), BF16),
        pltpu.VMEM((width, rows), BF16),
        pltpu.VMEM((8, Q, 2, per, rows), BF16),
        pltpu.VMEM((8, rows), F32),
        pltpu.VMEM((1, rows), F32),
        pltpu.VMEM((ITERS, 8, Q, 2, per, width), BF16),
        pltpu.VMEM((8, Q, per, width), F32),
        pltpu.VMEM((ITERS, 8, Q, per, width), BF16),
        pltpu.VMEM((ITERS, 8, Q, per, width), BF16),
        pltpu.VMEM((ITERS, 8, Q, per, width), BF16),
        pltpu.VMEM((ITERS, 3, Q, per, width), BF16),
        pltpu.VMEM((ITERS, Q, per, width), BF16),
        pltpu.VMEM((ITERS, 3, Q, per, width), BF16),
        pltpu.VMEM((Q, per, width), F32),
        pltpu.VMEM((rows, width), BF16),
        dma((N_SEMS,)), dma((N_SEMS,)), dma((16,)),
    ]
    anyspace = pl.BlockSpec(memory_space=pl.ANY)
    hbm = pl.BlockSpec(memory_space=pltpu.MemorySpace.HBM)
    shapes = (
        jax.ShapeDtypeStruct((1, mine, width), F32),
        jax.ShapeDtypeStruct((1, rows, width), BF16),
    )
    results = pl.pallas_call(
        kernel,
        out_shape=shapes,
        in_specs=[hbm, hbm, hbm],
        out_specs=(anyspace, anyspace),
        scratch_shapes=scratch,
        compiler_params=pltpu.CompilerParams(
            collective_id=0, has_side_effects=True, vmem_limit_bytes=VLIM * 1024 * 1024
        ),
    )(*[pltpu.with_memory_space_constraint(v, pltpu.MemorySpace.HBM) for v in (tile_counts, points, centroids)])
    return pl.pallas_call(
        flush,
        out_shape=shapes,
        in_specs=[anyspace, anyspace],
        out_specs=(hbm, hbm),
        scratch_shapes=[dma((5,))],
        compiler_params=pltpu.CompilerParams(vmem_limit_bytes=1024 * 1024),
    )(*results)


def solution(mesh):
    return jax.shard_map(
        body,
        mesh=mesh,
        in_specs=(P("grp", "shard", None), P("grp", "shard", None), P()),
        out_specs=(P("grp", "shard", None), P("grp", "shard", None)),
        check_vma=False,
    )
```

```python
import math

import jax
import jax.numpy as jnp
from jax import lax
from jax.experimental import pallas as pl
from jax.experimental.pallas import tpu as pltpu
from jax.sharding import PartitionSpec as P

MESH = pl.DeviceIdType.MESH
TILE = 128
ITERS = 2
EPS = 1e-06
SHARP = 48.0
Q = 4
F32 = jnp.float32
BF16 = jnp.bfloat16
N_SEMS = 224
VLIM = 40
UNROLL = 2
YO, ZP1, ZM1, OWN, ZZ = 0, 1, 2, 3, 4


def kernel(
    counts_in, points, cents, newc, post,
    counts, pts, n, nt, e, den, inv, tab, acc, ssnd, srcv, x, r1, r2, r3,
    send, recv, lsem,
):
    rows_all, width = n.shape
    per = tab.shape[4]
    g = lax.axis_index("grp")
    sh = lax.axis_index("shard")
    z, y, c = sh // 4, (sh // 2) % 2, sh % 2

    def peer(dz, dy, dc):
        zz = (z + dz) % 4
        yy = (y + dy) % 2
        cc = (c + dc) % 2
        return (g, zz * 4 + yy * 2 + cc)

    zp, zm, yo, sib = peer(1, 0, 0), peer(3, 0, 0), peer(0, 1, 0), peer(0, 0, 1)

    copies = {}
    drained = set()

    def start(key, src, dst, dev):
        i = len(copies)
        cp = pltpu.make_async_remote_copy(
            src_ref=src, dst_ref=dst, send_sem=send.at[i], recv_sem=recv.at[i],
            device_id=dev, device_id_type=MESH,
        )
        cp.start()
        copies[key] = cp

    def got(*key):
        copies[key].wait_recv()

    def drain():
        for key, cp in copies.items():
            if key not in drained:
                cp.wait_send()
                drained.add(key)

    parts = 4
    prow = rows_all // parts
    own_load = []
    for q in range(Q):
        cp = pltpu.make_async_copy(
            cents.at[0, pl.ds(q * per, per)], tab.at[0, OWN, q, 0], lsem.at[parts + q]
        )
        cp.start()
        own_load.append(cp)

    barrier = pltpu.get_barrier_semaphore()
    for dev in (zp, zm, yo, sib):
        pl.semaphore_signal(barrier, inc=1, device_id=dev, device_id_type=MESH)
    loads = []
    for i in range(parts):
        cp = pltpu.make_async_copy(
            points.at[0, pl.ds(i * prow, prow)], pts.at[pl.ds(i * prow, prow)], lsem.at[i]
        )
        cp.start()
        loads.append(cp)
    count_load = pltpu.make_async_copy(counts_in, counts, lsem.at[15])
    count_load.start()
    pl.semaphore_wait(barrier, 4)

    def hop(it, q, name, p, p_dst, dev):
        start((it, q, name), tab.at[it, p, q, 0], tab.at[it, p_dst, q, 0], dev)

    def ag_own(it, q):
        hop(it, q, "y", OWN, YO, yo)
        start((it, q, "s", OWN), tab.at[it, OWN, q, 0], tab.at[it, OWN, q, 1], sib)

    def ag_zp(it, q):
        hop(it, q, "zp", OWN, ZM1, zp)

    def ag_zm(it, q):
        hop(it, q, "zm", OWN, ZP1, zm)

    def share(it, q, p):
        start((it, q, "s", p), tab.at[it, p, q, 0], tab.at[it, p, q, 1], sib)

    def shared(it, pieces):
        for p, q in pieces:
            got(it, q, "s", p)

    def from_zp(it, q):
        got(it, q, "zp")
        if q >= 2:
            hop(it, q, "r6", ZM1, 6, yo)
        if q % 2 == 0:
            hop(it, q, "h", ZM1, ZZ, zp)
        share(it, q, ZM1)

    def from_zm(it, q):
        got(it, q, "zm")
        if q >= 2:
            hop(it, q, "r5", ZP1, 5, yo)
        if q % 2 == 1:
            hop(it, q, "h", ZP1, ZZ, zm)
        share(it, q, ZP1)

    def from_y(it, q):
        got(it, q, "y")
        if q < 2:
            hop(it, q, "r6", YO, 6, zp)
            hop(it, q, "r5", YO, 5, zm)
        share(it, q, YO)

    def from_h(it, q):
        got(it, q, "h")
        if q < 2:
            hop(it, q, "w", ZZ, 7, yo)
        share(it, q, ZZ)

    def from_side(it, q, p):
        got(it, q, "r%d" % p)
        if (q, p) == (2, 6):
            hop(it, q, "w", 6, 7, zp)
        if (q, p) == (3, 5):
            hop(it, q, "w", 5, 7, zm)
        share(it, q, p)

    def from_w(it, q):
        got(it, q, "w")
        share(it, q, 7)

    scale = SHARP / width * math.log2(math.e)
    n_rt = rows_all // 256

    def logits(it, pieces, t0=0, t1=n_rt, first=False):
        m = len(pieces) * 2 * per

        def step(rt, carry):
            at = pl.ds(pl.multiple_of(rt * 256, 256), 256)
            left = [tab[it, p, q].reshape(2 * per, width) for p, q in pieces]
            s = jnp.dot(jnp.concatenate(left, axis=0), nt[:, at], preferred_element_type=F32)
            ex = jnp.exp2(s * scale)
            part = jnp.sum(ex.reshape(m // 8, 8, 256), axis=0)
            den[:, at] = part if first else den[:, at] + part
            ex = ex.astype(BF16).reshape(len(pieces), 2, per, 256)
            for i, (p, q) in enumerate(pieces):
                e[p, q, :, :, at] = ex[i]
            return carry

        lax.fori_loop(t0, t1, step, 0, unroll=UNROLL)

    def invert():
        for t in range(rows_all // TILE):
            at = slice(t * TILE, (t + 1) * TILE)
            live = (t * 16 + sh < counts[g]).astype(F32)
            inv[:, at] = live / jnp.sum(den[:, at], axis=0, keepdims=True)

    def weigh(p0, p1, q0, q1):
        m = (p1 - p0) * (q1 - q0) * 2 * per

        def step(j, carry):
            at = pl.ds(pl.multiple_of(j * 256, 256), 256)
            v = e[p0:p1, q0:q1, :, :, at].reshape(m, 256) * inv[:, at].astype(BF16)
            e[p0:p1, q0:q1, :, :, at] = v.astype(BF16).reshape(p1 - p0, q1 - q0, 2, per, 256)
            return carry

        lax.fori_loop(0, n_rt, step, 0, unroll=2)

    n_ft = width // 256

    def sums(it, p0, p1, q0, q1, f0=0, f1=n_ft):
        m = (p1 - p0) * (q1 - q0) * 2 * per
        if f0 == 0:
            weigh(p0, p1, q0, q1)

        def step(ft, carry):
            at = pl.ds(pl.multiple_of(ft * 256, 256), 256)
            s = jnp.dot(
                e[p0:p1, q0:q1].reshape(m, rows_all), n[:, at], preferred_element_type=F32
            ).reshape(p1 - p0, q1 - q0, 2, per, 256)
            acc[p0:p1, q0:q1, :, at] = s[:, :, 0]
            ssnd[it, p0:p1, q0:q1, :, at] = s[:, :, 1].astype(BF16)
            return carry

        lax.fori_loop(f0, f1, step, 0, unroll=2)
        if f1 == n_ft:
            for q in range(q0, q1):
                start((it, q, "x", p0), ssnd.at[it, pl.ds(p0, p1 - p0), q], srcv.at[it, pl.ds(p0, p1 - p0), q], sib)

    def base(it, p, q):
        return acc[p, q] + srcv[it, p, q].astype(F32)

    def give(it, q, name, i, p, value, dst, dev):
        x[it, p, q] = value.astype(BF16)
        start((it, q, name, i), x.at[it, p, q], dst, dev)

    def add1(it, q, i):
        got(it, q, "r1", i)
        return r1[it, i, q].astype(F32)

    def rs_seven(it, q):
        got(it, q, "x", 7)
        dev = yo if q < 2 else (zm if q == 2 else zp)
        give(it, q, "r1", 2, 7, base(it, 7, q), r1.at[it, 2, q], dev)

    def rs_rest(it, q):
        got(it, q, "x", 5)
        if q != 3:
            give(it, q, "r1", 0, 5, base(it, 5, q), r1.at[it, 0, q], zp if q < 2 else yo)
        if q != 2:
            give(it, q, "r1", 1, 6, base(it, 6, q), r1.at[it, 1, q], zm if q < 2 else yo)

    def rs_mid(it, q):
        p, i = (6, 1) if q == 2 else (5, 0)
        give(it, q, "r1", i, p, base(it, p, q) + add1(it, q, 2), r1.at[it, i, q], yo)

    def rs_two(it, q):
        got(it, q, "x", 3)
        v = base(it, ZZ, q)
        if q < 2:
            v = v + add1(it, q, 2)
        give(it, q, "r2", 0, ZZ, v, r2.at[it, q], zm if q % 2 == 0 else zp)

    def to_owner(it, q, p, v):
        slot, dev = (1, zp) if p == ZP1 else (0, zm)
        give(it, q, "r3", slot, p, v, r3.at[it, slot, q], dev)

    def rs_early(it, q):
        got(it, q, "x", 0)
        p = ZP1 if q % 2 == 0 else ZM1
        v = base(it, p, q)
        if q >= 2:
            v = v + add1(it, q, 0 if p == ZP1 else 1)
        to_owner(it, q, p, v)

    def rs_y(it, q):
        v = base(it, YO, q)
        if q < 2:
            v = v + add1(it, q, 0) + add1(it, q, 1)
        give(it, q, "r3", 2, YO, v, r3.at[it, 2, q], yo)

    def rs_three(it, q):
        got(it, q, "r2", 0)
        p = ZM1 if q % 2 == 0 else ZP1
        v = base(it, p, q) + r2[it, q].astype(F32)
        if q >= 2:
            v = v + add1(it, q, 0 if p == ZP1 else 1)
        to_owner(it, q, p, v)

    def rs_last(it, q):
        s = base(it, OWN, q)
        for i in range(3):
            got(it, q, "r3", i)
            s = s + r3[it, i, q].astype(F32)
        return s * lax.rsqrt(jnp.mean(s * s, axis=-1, keepdims=True) + EPS)


    def post_tile(t):
        at = slice(t * 256, (t + 1) * 256)
        w = e[:, :, :, :, at].reshape(16 * Q * per, 256)
        post[0, at, :] = lax.dot_general(
            w, tab[ITERS - 1].reshape(16 * Q * per, width),
            (((0,), (0,)), ((), ())), preferred_element_type=F32,
        ).astype(BF16)

    for cp in own_load:
        cp.wait()
    for i in range(Q):
        ag_zp(0, (0, 2, 3, 1)[i])
        ag_zm(0, (1, 3, 2, 0)[i])
        ag_own(0, i)

    def unit(j, carry):
        at = pl.ds(pl.multiple_of(j * 32, 32), 32)
        v = pts[at, :].astype(F32)
        n[at, :] = (v * lax.rsqrt(jnp.mean(v * v, axis=-1, keepdims=True) + EPS)).astype(BF16)
        return carry

    for i in range(parts):
        loads[i].wait()
        lax.fori_loop(i * prow // 32, (i + 1) * prow // 32, unit, 0, unroll=2)
    count_load.wait()

    def turn(j, carry):
        at = pl.ds(pl.multiple_of(j * 128, 128), 128)
        nt[:, at] = n[at, :].T
        return carry


    for it in range(ITERS):
        last = it == ITERS - 1
        if it > 0:
            drain()
        from_zp(it, 0)
        from_zm(it, 1)
        from_y(it, 0)
        if it == 0:
            lax.fori_loop(0, rows_all // 256, turn, 0)
        from_zp(it, 2)
        from_zm(it, 3)
        from_y(it, 1)
        if it == 0:
            lax.fori_loop(rows_all // 256, rows_all // 128, turn, 0)
        from_zp(it, 3)
        from_zm(it, 2)
        from_y(it, 2)
        now = [(YO, 0), (YO, 1), (ZM1, 0), (ZM1, 2), (ZP1, 1), (ZP1, 3)]
        shared(it, now)
        logits(it, now, 0, 2, first=True)
        from_zp(it, 1)
        from_zm(it, 0)
        from_y(it, 3)
        logits(it, now, 2, 6, first=True)
        from_h(it, 0)
        from_h(it, 1)
        now = [(YO, 2), (YO, 3), (ZM1, 3), (ZM1, 1), (ZP1, 2), (ZP1, 0)]
        shared(it, now)
        logits(it, now, 0, 2)
        from_side(it, 2, 6)
        from_side(it, 0, 5)
        from_side(it, 0, 6)
        logits(it, now, 2, 6)
        from_side(it, 3, 5)
        from_h(it, 2)
        from_h(it, 3)
        now = [(OWN, 0), (OWN, 1), (OWN, 2), (OWN, 3), (ZZ, 0), (ZZ, 1)]
        shared(it, now)
        logits(it, now, 0, 4)
        from_side(it, 1, 5)
        from_side(it, 1, 6)
        from_side(it, 3, 6)
        logits(it, now, 4, 6)
        now = [(ZZ, 2), (ZZ, 3), (5, 0), (6, 0), (6, 2), (5, 3)]
        shared(it, now)
        logits(it, now, 0, 2)
        from_side(it, 2, 5)
        logits(it, now, 2, 6)
        from_w(it, 0)
        from_w(it, 2)
        now = [(5, 1), (6, 1), (6, 3), (5, 2)]
        shared(it, now)
        logits(it, now, 0, 4)
        from_w(it, 1)
        from_w(it, 3)
        logits(it, now, 4, 6)
        now = [(7, 0), (7, 1), (7, 2), (7, 3)]
        shared(it, now)
        logits(it, now)
        invert()

        def fill(t):
            if last:
                post_tile(t)

        sums(it, 7, 8, 0, 4)
        sums(it, 5, 7, 0, 4)
        for q in (2, 3, 0, 1):
            rs_seven(it, q)
        sums(it, 3, 5, 0, 4)
        for q in range(Q):
            rs_rest(it, q)
        sums(it, 0, 3, 0, 2)
        rs_two(it, 2)
        rs_two(it, 3)
        sums(it, 0, 3, 2, 4, 0, 2)
        rs_two(it, 0)
        rs_mid(it, 2)
        sums(it, 0, 3, 2, 4, 2, 4)
        rs_two(it, 1)
        rs_mid(it, 3)
        rs_early(it, 0)
        rs_early(it, 1)
        fill(0)
        rs_y(it, 0)
        rs_y(it, 1)
        rs_early(it, 2)
        rs_early(it, 3)
        rs_y(it, 2)
        rs_y(it, 3)
        fill(1)
        rs_three(it, 0)
        rs_three(it, 2)
        fill(2)
        rs_three(it, 1)
        rs_three(it, 3)
        fill(3)
        if last:
            drain()
        fill(4)
        fill(5)
        for q in (0, 2, 1, 3):
            s = rs_last(it, q)
            if last:
                newc[0, q * per:(q + 1) * per] = s
            else:
                tab[it + 1, OWN, q, 0] = s.astype(BF16)
                ag_zp(it + 1, q)
                ag_zm(it + 1, q)
                ag_own(it + 1, q)
    drain()


def flush(newc_in, post_in, newc, post, sems):
    rows = post.shape[1]
    parts = 4
    cut = rows // parts
    cps = [pltpu.make_async_copy(newc_in, newc, sems.at[parts])]
    for i in range(parts):
        at = pl.ds(i * cut, cut)
        cps.append(pltpu.make_async_copy(post_in.at[0, at], post.at[0, at], sems.at[i]))
    for cp in cps:
        cp.start()
    for cp in cps:
        cp.wait()


def body(points, centroids, tile_counts):
    rows, width = points.shape[1:]
    mine = centroids.shape[1]
    per = mine // Q
    dma = pltpu.SemaphoreType.DMA
    scratch = [
        pltpu.SMEM(tile_counts.shape, jnp.int32),
        pltpu.VMEM((rows, width), BF16),
        pltpu.VMEM((rows, width), BF16),
        pltpu.VMEM((width, rows), BF16),
        pltpu.VMEM((8, Q, 2, per, rows), BF16),
        pltpu.VMEM((8, rows), F32),
        pltpu.VMEM((1, rows), F32),
        pltpu.VMEM((ITERS, 8, Q, 2, per, width), BF16),
        pltpu.VMEM((8, Q, per, width), F32),
        pltpu.VMEM((ITERS, 8, Q, per, width), BF16),
        pltpu.VMEM((ITERS, 8, Q, per, width), BF16),
        pltpu.VMEM((ITERS, 8, Q, per, width), BF16),
        pltpu.VMEM((ITERS, 3, Q, per, width), BF16),
        pltpu.VMEM((ITERS, Q, per, width), BF16),
        pltpu.VMEM((ITERS, 3, Q, per, width), BF16),
        dma((N_SEMS,)), dma((N_SEMS,)), dma((16,)),
    ]
    anyspace = pl.BlockSpec(memory_space=pl.ANY)
    hbm = pl.BlockSpec(memory_space=pltpu.MemorySpace.HBM)
    shapes = (
        jax.ShapeDtypeStruct((1, mine, width), F32),
        jax.ShapeDtypeStruct((1, rows, width), BF16),
    )
    results = pl.pallas_call(
        kernel,
        out_shape=shapes,
        in_specs=[hbm, hbm, hbm],
        out_specs=(pl.BlockSpec(memory_space=pltpu.MemorySpace.VMEM),) * 2,
        scratch_shapes=scratch,
        compiler_params=pltpu.CompilerParams(
            collective_id=0, has_side_effects=True, vmem_limit_bytes=VLIM * 1024 * 1024
        ),
    )(*[pltpu.with_memory_space_constraint(v, pltpu.MemorySpace.HBM) for v in (tile_counts, points, centroids)])
    return pl.pallas_call(
        flush,
        out_shape=shapes,
        in_specs=[anyspace, anyspace],
        out_specs=(hbm, hbm),
        scratch_shapes=[dma((5,))],
        compiler_params=pltpu.CompilerParams(vmem_limit_bytes=1024 * 1024),
    )(*results)


def solution(mesh):
    return jax.shard_map(
        body,
        mesh=mesh,
        in_specs=(P("grp", "shard", None), P("grp", "shard", None), P()),
        out_specs=(P("grp", "shard", None), P("grp", "shard", None)),
        check_vma=False,
    )
```

```python
import math

import jax
import jax.numpy as jnp
from jax import lax
from jax.experimental import pallas as pl
from jax.experimental.pallas import tpu as pltpu
from jax.sharding import PartitionSpec as P

MESH = pl.DeviceIdType.MESH
TILE = 128
ITERS = 2
EPS = 1e-06
SHARP = 48.0
Q = 4
F32 = jnp.float32
BF16 = jnp.bfloat16
N_SEMS = 224
VLIM = 40
UNROLL = 2
YO, ZP1, ZM1, OWN, ZZ = 0, 1, 2, 3, 4


def kernel(
    counts_in, points, cents, newc, post,
    counts, pts, n, nt, e, den, inv, tab, acc, ssnd, srcv, x, r1, r2, r3,
    send, recv, lsem,
):
    rows_all, width = n.shape
    per = tab.shape[4]
    g = lax.axis_index("grp")
    sh = lax.axis_index("shard")
    z, y, c = sh // 4, (sh // 2) % 2, sh % 2

    def peer(dz, dy, dc):
        zz = (z + dz) % 4
        yy = (y + dy) % 2
        cc = (c + dc) % 2
        return (g, zz * 4 + yy * 2 + cc)

    zp, zm, yo, sib = peer(1, 0, 0), peer(3, 0, 0), peer(0, 1, 0), peer(0, 0, 1)

    copies = {}
    drained = set()

    def start(key, src, dst, dev):
        i = len(copies)
        cp = pltpu.make_async_remote_copy(
            src_ref=src, dst_ref=dst, send_sem=send.at[i], recv_sem=recv.at[i],
            device_id=dev, device_id_type=MESH,
        )
        cp.start()
        copies[key] = cp

    def got(*key):
        copies[key].wait_recv()

    def drain():
        for key, cp in copies.items():
            if key not in drained:
                cp.wait_send()
                drained.add(key)

    parts = 4
    prow = rows_all // parts
    own_load = []
    for q in range(Q):
        cp = pltpu.make_async_copy(
            cents.at[0, pl.ds(q * per, per)], tab.at[0, OWN, q, 0], lsem.at[parts + q]
        )
        cp.start()
        own_load.append(cp)

    barrier = pltpu.get_barrier_semaphore()
    for dev in (zp, zm, yo, sib):
        pl.semaphore_signal(barrier, inc=1, device_id=dev, device_id_type=MESH)
    loads = []
    for i in range(parts):
        cp = pltpu.make_async_copy(
            points.at[0, pl.ds(i * prow, prow)], pts.at[pl.ds(i * prow, prow)], lsem.at[i]
        )
        cp.start()
        loads.append(cp)
    count_load = pltpu.make_async_copy(counts_in, counts, lsem.at[15])
    count_load.start()
    pl.semaphore_wait(barrier, 4)

    def hop(it, q, name, p, p_dst, dev):
        start((it, q, name), tab.at[it, p, q, 0], tab.at[it, p_dst, q, 0], dev)

    def ag_own(it, q):
        hop(it, q, "y", OWN, YO, yo)
        start((it, q, "s", OWN), tab.at[it, OWN, q, 0], tab.at[it, OWN, q, 1], sib)

    def ag_zp(it, q):
        hop(it, q, "zp", OWN, ZM1, zp)

    def ag_zm(it, q):
        hop(it, q, "zm", OWN, ZP1, zm)

    def share(it, q, p):
        start((it, q, "s", p), tab.at[it, p, q, 0], tab.at[it, p, q, 1], sib)

    def shared(it, pieces):
        for p, q in pieces:
            got(it, q, "s", p)

    def from_zp(it, q):
        got(it, q, "zp")
        if q >= 2:
            hop(it, q, "r6", ZM1, 6, yo)
        if q % 2 == 0:
            hop(it, q, "h", ZM1, ZZ, zp)
        share(it, q, ZM1)

    def from_zm(it, q):
        got(it, q, "zm")
        if q >= 2:
            hop(it, q, "r5", ZP1, 5, yo)
        if q % 2 == 1:
            hop(it, q, "h", ZP1, ZZ, zm)
        share(it, q, ZP1)

    def from_y(it, q):
        got(it, q, "y")
        if q < 2:
            hop(it, q, "r6", YO, 6, zp)
            hop(it, q, "r5", YO, 5, zm)
        share(it, q, YO)

    def from_h(it, q):
        got(it, q, "h")
        if q < 2:
            hop(it, q, "w", ZZ, 7, yo)
        share(it, q, ZZ)

    def from_side(it, q, p):
        got(it, q, "r%d" % p)
        if (q, p) == (2, 6):
            hop(it, q, "w", 6, 7, zp)
        if (q, p) == (3, 5):
            hop(it, q, "w", 5, 7, zm)
        share(it, q, p)

    def from_w(it, q):
        got(it, q, "w")
        share(it, q, 7)

    scale = SHARP / width * math.log2(math.e)
    n_rt = rows_all // 256

    def logits(it, pieces, t0=0, t1=n_rt, first=False):
        m = len(pieces) * 2 * per

        def step(rt, carry):
            at = pl.ds(pl.multiple_of(rt * 256, 256), 256)
            left = [tab[it, p, q].reshape(2 * per, width) for p, q in pieces]
            s = jnp.dot(jnp.concatenate(left, axis=0), nt[:, at], preferred_element_type=F32)
            ex = jnp.exp2(s * scale)
            part = jnp.sum(ex.reshape(m // 8, 8, 256), axis=0)
            den[:, at] = part if first else den[:, at] + part
            ex = ex.astype(BF16).reshape(len(pieces), 2, per, 256)
            for i, (p, q) in enumerate(pieces):
                e[p, q, :, :, at] = ex[i]
            return carry

        lax.fori_loop(t0, t1, step, 0, unroll=UNROLL)

    def invert():
        for t in range(rows_all // TILE):
            at = slice(t * TILE, (t + 1) * TILE)
            live = (t * 16 + sh < counts[g]).astype(F32)
            inv[:, at] = live / jnp.sum(den[:, at], axis=0, keepdims=True)

    def weigh(p0, p1, q0, q1):
        m = (p1 - p0) * (q1 - q0) * 2 * per

        def step(j, carry):
            at = pl.ds(pl.multiple_of(j * 256, 256), 256)
            v = e[p0:p1, q0:q1, :, :, at].reshape(m, 256) * inv[:, at].astype(BF16)
            e[p0:p1, q0:q1, :, :, at] = v.astype(BF16).reshape(p1 - p0, q1 - q0, 2, per, 256)
            return carry

        lax.fori_loop(0, n_rt, step, 0, unroll=2)

    n_ft = width // 256

    def sums(it, p0, p1, q0, q1, f0=0, f1=n_ft):
        m = (p1 - p0) * (q1 - q0) * 2 * per
        if f0 == 0:
            weigh(p0, p1, q0, q1)

        def step(ft, carry):
            at = pl.ds(pl.multiple_of(ft * 256, 256), 256)
            s = jnp.dot(
                e[p0:p1, q0:q1].reshape(m, rows_all), n[:, at], preferred_element_type=F32
            ).reshape(p1 - p0, q1 - q0, 2, per, 256)
            acc[p0:p1, q0:q1, :, at] = s[:, :, 0]
            ssnd[it, p0:p1, q0:q1, :, at] = s[:, :, 1].astype(BF16)
            return carry

        lax.fori_loop(f0, f1, step, 0, unroll=2)
        if f1 == n_ft:
            for q in range(q0, q1):
                start((it, q, "x", p0), ssnd.at[it, pl.ds(p0, p1 - p0), q], srcv.at[it, pl.ds(p0, p1 - p0), q], sib)

    def base(it, p, q):
        return acc[p, q] + srcv[it, p, q].astype(F32)

    def give(it, q, name, i, p, value, dst, dev):
        x[it, p, q] = value.astype(BF16)
        start((it, q, name, i), x.at[it, p, q], dst, dev)

    def add1(it, q, i):
        got(it, q, "r1", i)
        return r1[it, i, q].astype(F32)

    def rs_seven(it, q):
        got(it, q, "x", 7)
        dev = yo if q < 2 else (zm if q == 2 else zp)
        give(it, q, "r1", 2, 7, base(it, 7, q), r1.at[it, 2, q], dev)

    def rs_rest(it, q):
        got(it, q, "x", 5)
        if q != 3:
            give(it, q, "r1", 0, 5, base(it, 5, q), r1.at[it, 0, q], zp if q < 2 else yo)
        if q != 2:
            give(it, q, "r1", 1, 6, base(it, 6, q), r1.at[it, 1, q], zm if q < 2 else yo)

    def rs_mid(it, q):
        p, i = (6, 1) if q == 2 else (5, 0)
        give(it, q, "r1", i, p, base(it, p, q) + add1(it, q, 2), r1.at[it, i, q], yo)

    def rs_two(it, q):
        got(it, q, "x", 3)
        v = base(it, ZZ, q)
        if q < 2:
            v = v + add1(it, q, 2)
        give(it, q, "r2", 0, ZZ, v, r2.at[it, q], zm if q % 2 == 0 else zp)

    def to_owner(it, q, p, v):
        slot, dev = (1, zp) if p == ZP1 else (0, zm)
        give(it, q, "r3", slot, p, v, r3.at[it, slot, q], dev)

    def rs_early(it, q):
        got(it, q, "x", 0)
        p = ZP1 if q % 2 == 0 else ZM1
        v = base(it, p, q)
        if q >= 2:
            v = v + add1(it, q, 0 if p == ZP1 else 1)
        to_owner(it, q, p, v)

    def rs_y(it, q):
        v = base(it, YO, q)
        if q < 2:
            v = v + add1(it, q, 0) + add1(it, q, 1)
        give(it, q, "r3", 2, YO, v, r3.at[it, 2, q], yo)

    def rs_three(it, q):
        got(it, q, "r2", 0)
        p = ZM1 if q % 2 == 0 else ZP1
        v = base(it, p, q) + r2[it, q].astype(F32)
        if q >= 2:
            v = v + add1(it, q, 0 if p == ZP1 else 1)
        to_owner(it, q, p, v)

    def rs_last(it, q):
        s = base(it, OWN, q)
        for i in range(3):
            got(it, q, "r3", i)
            s = s + r3[it, i, q].astype(F32)
        return s * lax.rsqrt(jnp.mean(s * s, axis=-1, keepdims=True) + EPS)


    def post_tile(t):
        at = slice(t * 256, (t + 1) * 256)
        w = e[:, :, :, :, at].reshape(16 * Q * per, 256)
        post[0, at, :] = lax.dot_general(
            w, tab[ITERS - 1].reshape(16 * Q * per, width),
            (((0,), (0,)), ((), ())), preferred_element_type=F32,
        ).astype(BF16)

    for cp in own_load:
        cp.wait()
    for i in range(Q):
        ag_zp(0, (0, 2, 3, 1)[i])
        ag_zm(0, (1, 3, 2, 0)[i])
        ag_own(0, i)

    def unit(j, carry):
        at = pl.ds(pl.multiple_of(j * 32, 32), 32)
        v = pts[at, :].astype(F32)
        n[at, :] = (v * lax.rsqrt(jnp.mean(v * v, axis=-1, keepdims=True) + EPS)).astype(BF16)
        return carry

    for i in range(parts):
        loads[i].wait()
        lax.fori_loop(i * prow // 32, (i + 1) * prow // 32, unit, 0, unroll=2)
    count_load.wait()

    def turn(j, carry):
        at = pl.ds(pl.multiple_of(j * 128, 128), 128)
        nt[:, at] = n[at, :].T
        return carry


    for it in range(ITERS):
        last = it == ITERS - 1
        if it > 0:
            drain()
        from_zp(it, 0)
        from_zm(it, 1)
        from_y(it, 0)
        if it == 0:
            lax.fori_loop(0, rows_all // 256, turn, 0)
        from_zp(it, 2)
        from_zm(it, 3)
        from_y(it, 1)
        if it == 0:
            lax.fori_loop(rows_all // 256, rows_all // 128, turn, 0)
        from_zp(it, 3)
        from_zm(it, 2)
        from_y(it, 2)
        now = [(YO, 0), (YO, 1), (ZM1, 0), (ZM1, 2), (ZP1, 1), (ZP1, 3)]
        shared(it, now)
        logits(it, now, 0, 2, first=True)
        from_zp(it, 1)
        from_zm(it, 0)
        from_y(it, 3)
        logits(it, now, 2, 6, first=True)
        from_h(it, 0)
        from_h(it, 1)
        now = [(YO, 2), (YO, 3), (ZM1, 3), (ZM1, 1), (ZP1, 2), (ZP1, 0)]
        shared(it, now)
        logits(it, now, 0, 2)
        from_side(it, 2, 6)
        from_side(it, 0, 5)
        from_side(it, 0, 6)
        logits(it, now, 2, 6)
        from_side(it, 3, 5)
        from_h(it, 2)
        from_h(it, 3)
        now = [(OWN, 0), (OWN, 1), (OWN, 2), (OWN, 3), (ZZ, 0), (ZZ, 1)]
        shared(it, now)
        logits(it, now, 0, 4)
        from_side(it, 1, 5)
        from_side(it, 1, 6)
        from_side(it, 3, 6)
        logits(it, now, 4, 6)
        now = [(ZZ, 2), (ZZ, 3), (5, 0), (6, 0), (6, 2), (5, 3)]
        shared(it, now)
        logits(it, now, 0, 2)
        from_side(it, 2, 5)
        logits(it, now, 2, 6)
        from_w(it, 0)
        from_w(it, 2)
        now = [(5, 1), (6, 1), (6, 3), (5, 2)]
        shared(it, now)
        logits(it, now, 0, 4)
        from_w(it, 1)
        from_w(it, 3)
        logits(it, now, 4, 6)
        now = [(7, 0), (7, 1), (7, 2), (7, 3)]
        shared(it, now)
        logits(it, now)
        invert()

        def fill(t):
            if last:
                post_tile(t)

        sums(it, 7, 8, 0, 4)
        sums(it, 5, 7, 0, 4)
        for q in (2, 3, 0, 1):
            rs_seven(it, q)
        sums(it, 3, 5, 0, 4)
        for q in range(Q):
            rs_rest(it, q)
        sums(it, 0, 3, 0, 2)
        rs_two(it, 2)
        rs_two(it, 3)
        sums(it, 0, 3, 2, 4, 0, 2)
        rs_two(it, 0)
        rs_mid(it, 2)
        sums(it, 0, 3, 2, 4, 2, 4)
        rs_two(it, 1)
        rs_mid(it, 3)
        rs_early(it, 0)
        rs_early(it, 1)
        rs_y(it, 0)
        fill(0)
        rs_y(it, 1)
        rs_early(it, 2)
        rs_early(it, 3)
        rs_y(it, 2)
        rs_y(it, 3)
        fill(1)
        rs_three(it, 0)
        rs_three(it, 2)
        fill(2)
        rs_three(it, 1)
        rs_three(it, 3)
        fill(3)
        if last:
            drain()
        fill(4)
        fill(5)
        for q in (0, 2, 1, 3):
            s = rs_last(it, q)
            if last:
                newc[0, q * per:(q + 1) * per] = s
            else:
                tab[it + 1, OWN, q, 0] = s.astype(BF16)
                ag_zp(it + 1, q)
                ag_zm(it + 1, q)
                ag_own(it + 1, q)
    drain()


def flush(newc_in, post_in, newc, post, sems):
    rows = post.shape[1]
    parts = 4
    cut = rows // parts
    cps = [pltpu.make_async_copy(newc_in, newc, sems.at[parts])]
    for i in range(parts):
        at = pl.ds(i * cut, cut)
        cps.append(pltpu.make_async_copy(post_in.at[0, at], post.at[0, at], sems.at[i]))
    for cp in cps:
        cp.start()
    for cp in cps:
        cp.wait()


def body(points, centroids, tile_counts):
    rows, width = points.shape[1:]
    mine = centroids.shape[1]
    per = mine // Q
    dma = pltpu.SemaphoreType.DMA
    scratch = [
        pltpu.SMEM(tile_counts.shape, jnp.int32),
        pltpu.VMEM((rows, width), BF16),
        pltpu.VMEM((rows, width), BF16),
        pltpu.VMEM((width, rows), BF16),
        pltpu.VMEM((8, Q, 2, per, rows), BF16),
        pltpu.VMEM((8, rows), F32),
        pltpu.VMEM((1, rows), F32),
        pltpu.VMEM((ITERS, 8, Q, 2, per, width), BF16),
        pltpu.VMEM((8, Q, per, width), F32),
        pltpu.VMEM((ITERS, 8, Q, per, width), BF16),
        pltpu.VMEM((ITERS, 8, Q, per, width), BF16),
        pltpu.VMEM((ITERS, 8, Q, per, width), BF16),
        pltpu.VMEM((ITERS, 3, Q, per, width), BF16),
        pltpu.VMEM((ITERS, Q, per, width), BF16),
        pltpu.VMEM((ITERS, 3, Q, per, width), BF16),
        dma((N_SEMS,)), dma((N_SEMS,)), dma((16,)),
    ]
    anyspace = pl.BlockSpec(memory_space=pl.ANY)
    hbm = pl.BlockSpec(memory_space=pltpu.MemorySpace.HBM)
    shapes = (
        jax.ShapeDtypeStruct((1, mine, width), F32),
        jax.ShapeDtypeStruct((1, rows, width), BF16),
    )
    results = pl.pallas_call(
        kernel,
        out_shape=shapes,
        in_specs=[hbm, hbm, hbm],
        out_specs=(pl.BlockSpec(memory_space=pltpu.MemorySpace.VMEM),) * 2,
        scratch_shapes=scratch,
        compiler_params=pltpu.CompilerParams(
            collective_id=0, has_side_effects=True, vmem_limit_bytes=VLIM * 1024 * 1024
        ),
    )(*[pltpu.with_memory_space_constraint(v, pltpu.MemorySpace.HBM) for v in (tile_counts, points, centroids)])
    return pl.pallas_call(
        flush,
        out_shape=shapes,
        in_specs=[anyspace, anyspace],
        out_specs=(hbm, hbm),
        scratch_shapes=[dma((5,))],
        compiler_params=pltpu.CompilerParams(vmem_limit_bytes=1024 * 1024),
    )(*results)


def solution(mesh):
    return jax.shard_map(
        body,
        mesh=mesh,
        in_specs=(P("grp", "shard", None), P("grp", "shard", None), P()),
        out_specs=(P("grp", "shard", None), P("grp", "shard", None)),
        check_vma=False,
    )
```
